128 devices in a mesh: row: 8 (over x_lo, y), col: 16 (over x_hi, z, core).
Axes of the slice: x: 4 (x_hi: 2, x_lo: 2; x = x_hi * 2 + x_lo), y: 4, z: 4, core: 2. Of those that a mesh axis runs over, the one named last changes fastest.
Arguments:
- sensitivity: bfloat16 [128, 8, 2, 256, 128], P(('row', 'col')), may hold values from -0.3984375 to 0.3984375
- tile_ids: int32 [128, 8, 2], P(('row', 'col')), may hold values from 0 to 15, as said below
- counts: int32 [128, 8], P(('row', 'col')), may hold values from 0 to 2, as said below
- weight_class: int32 [128, 256], P(('row', 'col')), may hold values from 0 to 3
Outputs:
- normal_matrix: float32 [16384, 16384], P('row', 'col')
The draws below stay inside these ranges and needn't reach their ends.
Inputs may be any that keep to these rules, and one draw needn't show every extreme that they name: `tile_ids`: within one station block and one row owner the 2 slots name distinct tiles. `counts`: slots at or beyond the count are padding; in every draw some station block uses all 2 slots of every row owner.
All inputs are finite; a program needn't handle non-finite values.
Results may differ from the reference program's by a relative error of at most 0.0003.
Values may be sent and summed in bfloat16 or wider, within the bound.
A program may use at most 128 MiB of HBM per device.

```python
import jax
import jax.numpy as jnp
from jax import lax

TILE = 128
TILES = 128
CAP = 2
ROWS = 256
BLOCKS = 128
N_ROW = 8


def draw_tile_ids(key, part):
    per_row = TILES // N_ROW
    scores = jax.random.randint(key, (BLOCKS, N_ROW, per_row), 0, 1 << 20) * per_row
    scores = scores + jnp.arange(per_row, dtype=jnp.int32)
    order = jnp.argsort(scores, axis=-1, stable=True)
    return order[..., :CAP].astype(jnp.int32)


def draw_counts(key, part):
    first, second = jax.random.split(jax.random.fold_in(key, 7))
    counts = jax.random.randint(first, (BLOCKS, N_ROW), 0, CAP + 1)
    chosen = jax.random.randint(second, (), 0, BLOCKS)
    full = jnp.arange(BLOCKS, dtype=jnp.int32)[:, None] == chosen
    return jnp.where(full, CAP, counts).astype(jnp.int32)


def with_ends(drawn, key, least, top_value):
    spot = [jax.random.randint(jax.random.fold_in(key, axis), (), 0, length) for axis, length in enumerate(drawn.shape)]
    widest = drawn.shape.index(max(drawn.shape))
    neighbour = spot[:widest] + [(spot[widest] + 1) % drawn.shape[widest]] + spot[widest + 1:]
    return drawn.at[tuple(spot)].set(least).at[tuple(neighbour)].set(top_value)


def shard_levels(stream_key, dims, cuts, smallest, largest):
    level = 1.0
    for axis_at, parts in cuts:
        steps = jax.random.uniform(jax.random.fold_in(jax.random.fold_in(stream_key, 6), axis_at), (parts,), jnp.float32, smallest / len(cuts), largest / len(cuts))
        level = level * jnp.repeat(jnp.exp(steps), dims[axis_at] // parts).reshape((-1,) + (1,) * (len(dims) - 1 - axis_at))
    return level


def centred(own_key, dims, scale, most, cuts=(), kind=jnp.bfloat16):
    gain = shard_levels(own_key, dims, cuts, -0.22, 0.18) if cuts else 1.0
    result = jax.random.normal(own_key, dims, jnp.float32) * scale * gain
    return jnp.minimum(jnp.maximum(result, -most), most).astype(kind)


def setup_inputs(seed: int = 0) -> dict:
    arg_keys = jax.random.split(jax.random.key(seed), 5)
    sensitivity = centred(arg_keys[0], (BLOCKS, N_ROW, CAP, ROWS, TILE), 0.05, 0.3984375, ((0, 128),))
    tile_ids = draw_tile_ids(jax.random.fold_in(arg_keys[4], 71), 0)
    counts = draw_counts(jax.random.fold_in(arg_keys[4], 71), 0)
    weight_class = with_ends(jax.random.randint(arg_keys[3], (BLOCKS, ROWS), 0, 4), jax.random.fold_in(arg_keys[3], 1), 0, 3).astype(jnp.int32)
    return dict(sensitivity=sensitivity, tile_ids=tile_ids, counts=counts, weight_class=weight_class)


def station_scale(weight_class):
    levels = jnp.array([1.0, 0.5, 0.25, 0.125], jnp.float32)
    hits = weight_class[..., None] == jnp.arange(4, dtype=jnp.int32)
    return jnp.sum(jnp.where(hits, levels, jnp.float32(0.0)), axis=-1)


def reference(sensitivity, tile_ids, counts, weight_class):
    blocks, row_devices, slots, rows, width = sensitivity.shape
    per_row = TILES // row_devices
    live = jnp.arange(slots, dtype=jnp.int32)[None, None, :] < counts[:, :, None]
    factor = station_scale(weight_class)[:, None, None, :, None] * live[:, :, :, None, None].astype(jnp.float32)
    weighted = (sensitivity.astype(jnp.float32) * factor).astype(jnp.bfloat16)
    offsets = (jnp.arange(row_devices, dtype=jnp.int32) * per_row)[None, :, None]
    global_ids = (tile_ids + offsets).astype(jnp.int32).reshape(blocks, row_devices * slots)
    compact = jnp.transpose(weighted, (0, 3, 1, 2, 4)).reshape(blocks, rows, row_devices * slots * width)
    count_slots = row_devices * slots

    def add_block(index, normal):
        left = lax.dynamic_index_in_dim(compact, index, 0, keepdims=False)
        gram = jnp.dot(left.T, left, preferred_element_type=jnp.float32)
        gram = jnp.transpose(gram.reshape(count_slots, width, count_slots, width), (0, 2, 1, 3))
        ids = lax.dynamic_index_in_dim(global_ids, index, 0, keepdims=False)
        return normal.at[ids[:, None], :, ids[None, :], :].add(gram)

    normal = jnp.zeros((TILES, width, TILES, width), jnp.float32)
    normal = lax.fori_loop(0, blocks, add_block, normal)
    return normal.reshape(TILES * width, TILES * width)
```

```python
import functools

import jax
import jax.numpy as jnp
from jax import lax
from jax.experimental import pallas as pl
from jax.experimental.pallas import tpu as pltpu
from jax.sharding import PartitionSpec as P

TILES = 128
GROUP = 8


def station_scale(weight_class):
    levels = jnp.array([1.0, 0.5, 0.25, 0.125], jnp.float32)
    hits = weight_class[..., None] == jnp.arange(4, dtype=jnp.int32)
    return jnp.sum(jnp.where(hits, levels, jnp.float32(0.0)), axis=-1)


def gram_kernel(slots, width, lids_ref, rids_ref, left_ref, right_ref, out_ref):
    g = pl.program_id(0)

    @pl.when(g == 0)
    def _():
        out_ref[...] = jnp.zeros_like(out_ref)

    def body(k, carry):
        b = g * GROUP + k
        for i in range(slots):
            li = lids_ref[b * slots + i]
            for j in range(slots):
                rj = rids_ref[b * slots + j]

                @pl.when((li >= 0) & (rj >= 0))
                def _():
                    prod = lax.dot_general(
                        left_ref[k, i],
                        right_ref[k, j],
                        (((0,), (0,)), ((), ())),
                        preferred_element_type=jnp.float32,
                    )
                    rows = pl.ds(pl.multiple_of(li * width, width), width)
                    cols = pl.ds(pl.multiple_of(rj * width, width), width)
                    out_ref[rows, cols] += prod

        return carry

    lax.fori_loop(0, GROUP, body, 0)


def accumulate(left_data, left_ids, right_data, right_ids, per_row, per_col):
    stations, slots, rows, width = left_data.shape
    block = (GROUP, slots, rows, width)
    grid_spec = pltpu.PrefetchScalarGridSpec(
        num_scalar_prefetch=2,
        grid=(stations // GROUP,),
        in_specs=[
            pl.BlockSpec(block, lambda g, lids, rids: (g, 0, 0, 0)),
            pl.BlockSpec(block, lambda g, lids, rids: (g, 0, 0, 0)),
        ],
        out_specs=pl.BlockSpec((per_row * width, per_col * width), lambda g, lids, rids: (0, 0)),
    )
    flops = 2 * stations * slots * slots * rows * width * width
    return pl.pallas_call(
        functools.partial(gram_kernel, slots, width),
        grid_spec=grid_spec,
        out_shape=jax.ShapeDtypeStruct((per_row * width, per_col * width), jnp.float32),
        compiler_params=pltpu.CompilerParams(
            dimension_semantics=("arbitrary",), vmem_limit_bytes=48 * 1024 * 1024
        ),
        cost_estimate=pl.CostEstimate(
            flops=flops,
            bytes_accessed=2 * left_data.size * 2 + per_row * per_col * width * width * 4,
            transcendentals=0,
        ),
    )(left_ids.reshape(-1), right_ids.reshape(-1), left_data, right_data)


def local(sensitivity, tile_ids, counts, weight_class):
    row_devices = lax.axis_size("row")
    col_devices = lax.axis_size("col")
    blocks, _, slots, rows, width = sensitivity.shape
    per_row = TILES // row_devices
    per_col = TILES // col_devices
    ratio = col_devices // row_devices
    live = jnp.arange(slots, dtype=jnp.int32)[None, None, :] < counts[:, :, None]
    factor = station_scale(weight_class)[:, None, None, :, None] * live[:, :, :, None, None].astype(
        jnp.float32
    )
    weighted = (sensitivity.astype(jnp.float32) * factor).astype(jnp.bfloat16)
    left_ids = jnp.where(live, tile_ids, -1)
    owned_data, owned_ids = (
        lax.all_to_all(weighted, "row", split_axis=1, concat_axis=0, tiled=True),
        lax.all_to_all(left_ids, "row", split_axis=1, concat_axis=0, tiled=True),
    )
    left_data, left_tiles = (
        lax.all_gather(owned_data, "col", axis=1, tiled=True),
        lax.all_gather(owned_ids, "col", axis=1, tiled=True),
    )
    stations = row_devices * col_devices * blocks
    left_data = left_data.reshape(stations, slots, rows, width)
    left_tiles = left_tiles.reshape(stations, slots)
    picked = jnp.repeat(weighted, ratio, axis=1)
    picked_ids = jnp.repeat(left_ids, ratio, axis=1)
    offsets = (jnp.arange(col_devices, dtype=jnp.int32) % ratio * per_col)[None, :, None]
    inside = (picked_ids >= offsets) & (picked_ids < offsets + per_col)
    chosen_ids = jnp.where(inside, picked_ids - offsets, -1)
    sorted_data, sorted_ids = (
        lax.all_to_all(picked, "col", split_axis=1, concat_axis=0, tiled=True),
        lax.all_to_all(chosen_ids, "col", split_axis=1, concat_axis=0, tiled=True),
    )
    right_data, right_tiles = (
        lax.all_gather(sorted_data, "row", axis=0, tiled=True),
        lax.all_gather(sorted_ids, "row", axis=0, tiled=True),
    )
    right_data = right_data.reshape(stations, slots, rows, width)
    right_tiles = right_tiles.reshape(stations, slots)
    return accumulate(left_data, left_tiles, right_data, right_tiles, per_row, per_col)


def solution(mesh):
    in_specs = (
        P(("row", "col"), None, None, None, None),
        P(("row", "col"), None, None),
        P(("row", "col"), None),
        P(("row", "col"), None),
    )
    out_specs = P("row", "col")
    return jax.shard_map(local, mesh=mesh, in_specs=in_specs, out_specs=out_specs, check_vma=False)
```

```python
import functools

import jax
import jax.numpy as jnp
from jax import lax
from jax.experimental import pallas as pl
from jax.experimental.pallas import tpu as pltpu
from jax.sharding import PartitionSpec as P

TILES = 128
GROUP = 8


def station_scale(weight_class):
    levels = jnp.array([1.0, 0.5, 0.25, 0.125], jnp.float32)
    hits = weight_class[..., None] == jnp.arange(4, dtype=jnp.int32)
    return jnp.sum(jnp.where(hits, levels, jnp.float32(0.0)), axis=-1)


def gram_kernel(slots, width, lids_ref, rids_ref, left_ref, right_ref, out_ref):
    g = pl.program_id(0)

    @pl.when(g == 0)
    def _():
        out_ref[...] = jnp.zeros_like(out_ref)

    def body(k, carry):
        b = g * GROUP + k
        for i in range(slots):
            li = lids_ref[b * slots + i]
            for j in range(slots):
                rj = rids_ref[b * slots + j]

                @pl.when((li >= 0) & (rj >= 0))
                def _():
                    prod = lax.dot_general(
                        left_ref[k, i],
                        right_ref[k, j],
                        (((0,), (0,)), ((), ())),
                        preferred_element_type=jnp.float32,
                    )
                    rows = pl.ds(pl.multiple_of(li * width, width), width)
                    cols = pl.ds(pl.multiple_of(rj * width, width), width)
                    out_ref[rows, cols] += prod

        return carry

    lax.fori_loop(0, GROUP, body, 0)


def accumulate(left_data, left_ids, right_data, right_ids, per_row, per_col):
    stations, slots, rows, width = left_data.shape
    block = (GROUP, slots, rows, width)
    grid_spec = pltpu.PrefetchScalarGridSpec(
        num_scalar_prefetch=2,
        grid=(stations // GROUP,),
        in_specs=[
            pl.BlockSpec(block, lambda g, lids, rids: (g, 0, 0, 0)),
            pl.BlockSpec(block, lambda g, lids, rids: (g, 0, 0, 0)),
        ],
        out_specs=pl.BlockSpec((per_row * width, per_col * width), lambda g, lids, rids: (0, 0)),
    )
    flops = 2 * stations * slots * slots * rows * width * width
    return pl.pallas_call(
        functools.partial(gram_kernel, slots, width),
        grid_spec=grid_spec,
        out_shape=jax.ShapeDtypeStruct((per_row * width, per_col * width), jnp.float32),
        compiler_params=pltpu.CompilerParams(
            dimension_semantics=("arbitrary",), vmem_limit_bytes=48 * 1024 * 1024
        ),
        cost_estimate=pl.CostEstimate(
            flops=flops,
            bytes_accessed=2 * left_data.size * 2 + per_row * per_col * width * width * 4,
            transcendentals=0,
        ),
    )(left_ids.reshape(-1), right_ids.reshape(-1), left_data, right_data)


def local(sensitivity, tile_ids, counts, weight_class):
    row_devices = lax.axis_size("row")
    chips = lax.axis_size("chip")
    cores = lax.axis_size("core")
    me_row = lax.axis_index("row")
    me_chip = lax.axis_index("chip")
    me_core = lax.axis_index("core")
    blocks, _, slots, rows, width = sensitivity.shape
    per_row = TILES // row_devices
    per_col = per_row // cores
    live = jnp.arange(slots, dtype=jnp.int32)[None, None, :] < counts[:, :, None]
    factor = station_scale(weight_class)[:, None, None, :, None] * live[:, :, :, None, None].astype(
        jnp.float32
    )
    weighted = (sensitivity.astype(jnp.float32) * factor).astype(jnp.bfloat16)
    live_ids = jnp.where(live, tile_ids, -1)
    all_ids = lax.all_gather(live_ids, ("row", "chip", "core"), axis=0, tiled=True)

    left = lax.all_to_all(weighted, "row", split_axis=1, concat_axis=0, tiled=True)
    left = lax.all_gather(left, "chip", axis=1, tiled=True)
    left = lax.all_gather(left, "core", axis=0, tiled=False)
    right = lax.all_to_all(weighted, "chip", split_axis=1, concat_axis=1, tiled=True)
    right = lax.all_gather(right, "row", axis=0, tiled=True)
    right = lax.all_gather(right, "core", axis=0, tiled=False)

    stations = row_devices * chips * cores * blocks
    left = left.reshape(stations, slots, rows, width)
    right = right.reshape(stations, slots, rows, width)
    order = (
        jnp.arange(row_devices, dtype=jnp.int32)[None, :, None] * (chips * cores)
        + jnp.arange(chips, dtype=jnp.int32)[None, None, :] * cores
        + jnp.arange(cores, dtype=jnp.int32)[:, None, None]
    ).reshape(-1)
    picked = all_ids[order]
    left_ids = picked[:, me_row, :]
    right_ids = picked[:, me_chip, :] - me_core * per_col
    right_ids = jnp.where((right_ids >= 0) & (right_ids < per_col), right_ids, -1)
    return accumulate(left, left_ids, right, right_ids, per_row, per_col)


def solution(mesh):
    row_devices, col_devices = mesh.devices.shape
    cores = 2
    mesh3 = jax.sharding.Mesh(
        mesh.devices.reshape(row_devices, col_devices // cores, cores), ("row", "chip", "core")
    )
    blocks = ("row", "chip", "core")
    in_specs = (
        P(blocks, None, None, None, None),
        P(blocks, None, None),
        P(blocks, None),
        P(blocks, None),
    )
    out_specs = P("row", ("chip", "core"))
    return jax.shard_map(local, mesh=mesh3, in_specs=in_specs, out_specs=out_specs, check_vma=False)
```

```python
import functools

import jax
import jax.numpy as jnp
from jax import lax
from jax.experimental import pallas as pl
from jax.experimental.pallas import tpu as pltpu
from jax.sharding import PartitionSpec as P

TILES = 128
BAND = 16


def station_scale(weight_class):
    levels = jnp.array([1.0, 0.5, 0.25, 0.125], jnp.float32)
    hits = weight_class[..., None] == jnp.arange(4, dtype=jnp.int32)
    return jnp.sum(jnp.where(hits, levels, jnp.float32(0.0)), axis=-1)


def gram_kernel(slots, rows, width, group, lids_ref, rids_ref, left_ref, right_ref, out_ref):
    co = pl.program_id(0)
    r = pl.program_id(1)

    @pl.when((co == 0) & (r == 0))
    def _():
        out_ref[...] = jnp.zeros_like(out_ref)

    base = (co * pl.num_programs(1) + r) * group

    def body(k, carry):
        b = base + k
        for i in range(slots):
            li = lids_ref[b * slots + i]
            for j in range(slots):
                rj = rids_ref[b * slots + j]

                @pl.when((li >= 0) & (rj >= 0))
                def _():
                    prod = lax.dot_general(
                        left_ref[k, i, :rows, :],
                        right_ref[k, j, :rows, :],
                        (((0,), (0,)), ((), ())),
                        preferred_element_type=jnp.float32,
                    )
                    out_rows = pl.ds(pl.multiple_of(li * width, width), width)
                    out_cols = pl.ds(pl.multiple_of(rj * width, width), width)
                    out_ref[out_rows, out_cols] += prod

        return carry

    lax.fori_loop(0, group, body, 0)


def accumulate(left, left_ids, right, right_ids, rows, per_row, per_col):
    n_row, n_chip, n_core, slots, band_rows, width = left.shape
    block = (None, n_chip, None, slots, band_rows, width)
    grid_spec = pltpu.PrefetchScalarGridSpec(
        num_scalar_prefetch=2,
        grid=(n_core, n_row),
        in_specs=[
            pl.BlockSpec(block, lambda co, r, lids, rids: (r, 0, co, 0, 0, 0)),
            pl.BlockSpec((None, None, n_chip, slots, band_rows, width), lambda co, r, lids, rids: (co, r, 0, 0, 0, 0)),
        ],
        out_specs=pl.BlockSpec((per_row * width, per_col * width), lambda co, r, lids, rids: (0, 0)),
    )
    stations = n_row * n_chip * n_core
    flops = 2 * stations * slots * slots * rows * width * width
    return pl.pallas_call(
        functools.partial(gram_kernel, slots, rows, width, n_chip),
        grid_spec=grid_spec,
        out_shape=jax.ShapeDtypeStruct((per_row * width, per_col * width), jnp.float32),
        compiler_params=pltpu.CompilerParams(
            dimension_semantics=("arbitrary", "arbitrary"), vmem_limit_bytes=48 * 1024 * 1024
        ),
        cost_estimate=pl.CostEstimate(
            flops=flops,
            bytes_accessed=2 * left.size * 2 + per_row * per_col * width * width * 4,
            transcendentals=0,
        ),
    )(left_ids.reshape(-1), right_ids.reshape(-1), left, right)


def local(sensitivity, tile_ids, counts, weight_class):
    row_devices = lax.axis_size("row")
    chips = lax.axis_size("chip")
    cores = lax.axis_size("core")
    me_core = lax.axis_index("core")
    blocks, owners, slots, rows, width = sensitivity.shape
    per_row = TILES // row_devices
    per_col = per_row // cores
    live = jnp.arange(slots, dtype=jnp.int32)[None, None, :] < counts[:, :, None]
    factor = station_scale(weight_class)[:, None, None, :, None] * live[:, :, :, None, None].astype(
        jnp.float32
    )
    weighted = (sensitivity.astype(jnp.float32) * factor).astype(jnp.bfloat16)
    live_ids = jnp.where(live, tile_ids, -1).astype(jnp.bfloat16)
    band = jnp.zeros((blocks, owners, slots, BAND, width), jnp.bfloat16)
    band = band.at[:, :, :, 0, :].set(live_ids[..., None])
    tagged = jnp.concatenate([weighted, band], axis=3)
    band_rows = rows + BAND

    left = lax.all_to_all(tagged, "row", split_axis=1, concat_axis=0, tiled=True)
    left = lax.all_gather(left, ("chip", "core"), axis=1, tiled=True)
    left = left.reshape(row_devices, chips, cores, slots, band_rows, width)
    right = lax.all_to_all(tagged, "chip", split_axis=1, concat_axis=1, tiled=True)
    right = lax.all_gather(right, "row", axis=0, tiled=True)
    right = lax.all_gather(right, "core", axis=0, tiled=False)
    right = right.reshape(cores, row_devices, chips, slots, band_rows, width)

    left_ids = jnp.transpose(left[:, :, :, :, rows, 0], (2, 0, 1, 3)).astype(jnp.int32)
    right_ids = right[:, :, :, :, rows, 0].astype(jnp.int32) - me_core * per_col
    right_ids = jnp.where((right_ids >= 0) & (right_ids < per_col), right_ids, -1)
    return accumulate(left, left_ids, right, right_ids, rows, per_row, per_col)


def solution(mesh):
    row_devices, col_devices = mesh.devices.shape
    cores = 2
    mesh3 = jax.sharding.Mesh(
        mesh.devices.reshape(row_devices, col_devices // cores, cores), ("row", "chip", "core")
    )
    blocks = ("row", "chip", "core")
    in_specs = (
        P(blocks, None, None, None, None),
        P(blocks, None, None),
        P(blocks, None),
        P(blocks, None),
    )
    out_specs = P("row", ("chip", "core"))
    return jax.shard_map(local, mesh=mesh3, in_specs=in_specs, out_specs=out_specs, check_vma=False)
```

```python
import functools

import jax
import jax.numpy as jnp
from jax import lax
from jax.experimental import pallas as pl
from jax.experimental.pallas import tpu as pltpu
from jax.sharding import PartitionSpec as P

TILES = 128
BAND = 16


def station_scale(weight_class):
    levels = jnp.array([1.0, 0.5, 0.25, 0.125], jnp.float32)
    hits = weight_class[..., None] == jnp.arange(4, dtype=jnp.int32)
    return jnp.sum(jnp.where(hits, levels, jnp.float32(0.0)), axis=-1)


def gram_kernel(slots, rows, width, group, carry_in, lids_ref, rids_ref, rot_ref, *refs):
    if carry_in:
        prev_ref, left_ref, right_ref, out_ref = refs
    else:
        left_ref, right_ref, out_ref = refs
    r = pl.program_id(0)

    @pl.when(r == 0)
    def _():
        if carry_in:
            out_ref[...] = prev_ref[...]
        else:
            out_ref[...] = jnp.zeros_like(out_ref)

    def body(k, carry):
        b = r * group + k
        for i in range(slots):
            li = lids_ref[b * slots + i]
            for j in range(slots):
                rj = rids_ref[b * slots + j]

                @pl.when((li >= 0) & (rj >= 0))
                def _():
                    prod = lax.dot_general(
                        left_ref[k, i, :rows, :],
                        right_ref[k, j, :rows, :],
                        (((0,), (0,)), ((), ())),
                        preferred_element_type=jnp.float32,
                    )
                    out_rows = pl.ds(pl.multiple_of(li * width, width), width)
                    out_cols = pl.ds(pl.multiple_of(rj * width, width), width)
                    out_ref[out_rows, out_cols] += prod

        return carry

    lax.fori_loop(0, group, body, 0)


def accumulate(prev, left, left_ids, right, right_ids, rot, rows, per_row, per_col):
    n_row, n_chip, n_core, slots, band_rows, width = left.shape
    n_y = right.shape[0]
    out_shape = (per_row * width, per_col * width)

    def right_map(r, lids, rids, rot):
        return (lax.rem(lax.rem(r, n_y) - rot[0] + n_y, n_y), r // n_y, 0, 0, 0, 0)

    in_specs = [
        pl.BlockSpec((None, n_chip, None, slots, band_rows, width), lambda r, lids, rids, rot: (r, 0, rot[1], 0, 0, 0)),
        pl.BlockSpec((None, None, n_chip, slots, band_rows, width), right_map),
    ]
    operands = [left, right]
    carry_in = prev is not None
    if carry_in:
        in_specs = [pl.BlockSpec(out_shape, lambda r, lids, rids, rot: (0, 0))] + in_specs
        operands = [prev] + operands
    grid_spec = pltpu.PrefetchScalarGridSpec(
        num_scalar_prefetch=3,
        grid=(n_row,),
        in_specs=in_specs,
        out_specs=pl.BlockSpec(out_shape, lambda r, lids, rids, rot: (0, 0)),
    )
    stations = n_row * n_chip
    flops = 2 * stations * slots * slots * rows * width * width
    return pl.pallas_call(
        functools.partial(gram_kernel, slots, rows, width, n_chip, carry_in),
        grid_spec=grid_spec,
        out_shape=jax.ShapeDtypeStruct(out_shape, jnp.float32),
        input_output_aliases={3: 0} if carry_in else {},
        compiler_params=pltpu.CompilerParams(
            dimension_semantics=("arbitrary",), vmem_limit_bytes=56 * 1024 * 1024
        ),
        cost_estimate=pl.CostEstimate(
            flops=flops,
            bytes_accessed=2 * right.size * 2 + per_row * per_col * width * width * 4,
            transcendentals=0,
        ),
    )(left_ids.reshape(-1), right_ids.reshape(-1), rot, *operands)

def shift(x, axis, step):
    n = lax.axis_size(axis)
    return lax.ppermute(x, axis, [(i, (i + step) % n) for i in range(n)])


def ring_gather(piece):
    other = shift(piece, "xlo", 1)
    first = lax.axis_index("xlo") == 0
    bundle = jnp.where(first, jnp.stack([piece, other]), jnp.stack([other, piece]))
    from_below = shift(bundle, "y", 1)
    from_above = shift(bundle, "y", -1)
    far_low = shift(from_below[:1], "y", 1)
    far_high = shift(from_above[1:], "y", -1)
    far = jnp.concatenate([far_low, far_high], axis=0)
    return jnp.stack([bundle, from_above, far, from_below])


def local(sensitivity, tile_ids, counts, weight_class):
    row_devices = lax.axis_size("xlo") * lax.axis_size("y")
    chips = lax.axis_size("chip")
    cores = lax.axis_size("core")
    me_core = lax.axis_index("core")
    blocks, owners, slots, rows, width = sensitivity.shape
    per_row = TILES // row_devices
    per_col = per_row // cores
    live = jnp.arange(slots, dtype=jnp.int32)[None, None, :] < counts[:, :, None]
    factor = station_scale(weight_class)[:, None, None, :, None] * live[:, :, :, None, None].astype(
        jnp.float32
    )
    weighted = (sensitivity.astype(jnp.float32) * factor).astype(jnp.bfloat16)
    live_ids = jnp.where(live, tile_ids, -1).astype(jnp.bfloat16)
    band = jnp.zeros((blocks, owners, slots, BAND, width), jnp.bfloat16)
    band = band.at[:, :, :, 0, :].set(live_ids[..., None])
    tagged = jnp.concatenate([weighted, band], axis=3)
    band_rows = rows + BAND

    left = lax.all_to_all(tagged, ("xlo", "y"), split_axis=1, concat_axis=0, tiled=True)
    left, tagged = lax.optimization_barrier((left, tagged))
    left = lax.all_gather(left, ("chip", "core"), axis=1, tiled=True)
    left = left.reshape(row_devices, chips, cores, slots, band_rows, width)
    right = lax.all_to_all(tagged, "chip", split_axis=1, concat_axis=1, tiled=True)
    right_own = ring_gather(right[0])
    right_other = shift(right_own, "core", 1)

    n_y = lax.axis_size("y")
    me_y = lax.axis_index("y")
    absolute_y = (jnp.arange(n_y, dtype=jnp.int32) - me_y) % n_y
    band_ids = left[:, :, :, :, rows, 0].astype(jnp.int32)

    def part(prev, right_half, core):
        left_ids = band_ids[:, :, core]
        right_ids = right_half[:, :, :, :, rows, 0].astype(jnp.int32) - me_core * per_col
        right_ids = jnp.transpose(right_ids[absolute_y], (1, 0, 2, 3))
        right_ids = jnp.where((right_ids >= 0) & (right_ids < per_col), right_ids, -1)
        rot = jnp.stack([me_y, core]).astype(jnp.int32)
        return accumulate(prev, left, left_ids, right_half, right_ids, rot, rows, per_row, per_col)

    normal = part(None, right_own, me_core)
    return part(normal, right_other, 1 - me_core)

def solution(mesh):
    row_devices, col_devices = mesh.devices.shape
    cores = 2
    x_lo = 2
    mesh3 = jax.sharding.Mesh(
        mesh.devices.reshape(x_lo, row_devices // x_lo, col_devices // cores, cores),
        ("xlo", "y", "chip", "core"),
    )
    blocks = ("xlo", "y", "chip", "core")
    in_specs = (
        P(blocks, None, None, None, None),
        P(blocks, None, None),
        P(blocks, None),
        P(blocks, None),
    )
    out_specs = P(("xlo", "y"), ("chip", "core"))
    return jax.shard_map(local, mesh=mesh3, in_specs=in_specs, out_specs=out_specs, check_vma=False)
```

```python
import functools

import jax
import jax.numpy as jnp
from jax import lax
from jax.experimental import pallas as pl
from jax.experimental.pallas import tpu as pltpu
from jax.sharding import PartitionSpec as P

TILES = 128
BAND = 16


def station_scale(weight_class):
    levels = jnp.array([1.0, 0.5, 0.25, 0.125], jnp.float32)
    hits = weight_class[..., None] == jnp.arange(4, dtype=jnp.int32)
    return jnp.sum(jnp.where(hits, levels, jnp.float32(0.0)), axis=-1)


def gram_kernel(slots, rows, width, group, carry_in, lids_ref, rids_ref, rot_ref, *refs):
    if carry_in:
        prev_ref, left_ref, right_ref, out_ref = refs
    else:
        left_ref, right_ref, out_ref = refs
    r = pl.program_id(0)

    @pl.when(r == 0)
    def _():
        if carry_in:
            out_ref[...] = prev_ref[...]
        else:
            out_ref[...] = jnp.zeros_like(out_ref)

    n_z = left_ref.shape[1]

    def body(k, carry):
        b = r * group + k
        x_rel = k // n_z
        z_rel = lax.rem(k, n_z)
        chip = lax.rem(rot_ref[1] + x_rel, 2) * n_z + lax.rem(rot_ref[2] + z_rel, n_z)
        for i in range(slots):
            li = lids_ref[b * slots + i]
            for j in range(slots):
                rj = rids_ref[b * slots + j]

                @pl.when((li >= 0) & (rj >= 0))
                def _():
                    prod = lax.dot_general(
                        left_ref[x_rel, z_rel, i, :rows, :],
                        right_ref[chip, j, :rows, :],
                        (((0,), (0,)), ((), ())),
                        preferred_element_type=jnp.float32,
                    )
                    out_rows = pl.ds(pl.multiple_of(li * width, width), width)
                    out_cols = pl.ds(pl.multiple_of(rj * width, width), width)
                    out_ref[out_rows, out_cols] += prod

        return carry

    lax.fori_loop(0, group, body, 0)


def accumulate(prev, left, left_ids, right, right_ids, rot, rows, per_row, per_col):
    n_xhi, n_z, n_row, slots, band_rows, width = left.shape
    n_chip = n_xhi * n_z
    n_y = right.shape[0]
    out_shape = (per_row * width, per_col * width)

    def right_map(r, lids, rids, rot):
        return (lax.rem(lax.rem(r, n_y) - rot[0] + n_y, n_y), r // n_y, 0, 0, 0, 0)

    in_specs = [
        pl.BlockSpec((n_xhi, n_z, None, slots, band_rows, width), lambda r, lids, rids, rot: (0, 0, r, 0, 0, 0)),
        pl.BlockSpec((None, None, n_chip, slots, band_rows, width), right_map),
    ]
    operands = [left, right]
    carry_in = prev is not None
    if carry_in:
        in_specs = [pl.BlockSpec(out_shape, lambda r, lids, rids, rot: (0, 0))] + in_specs
        operands = [prev] + operands
    grid_spec = pltpu.PrefetchScalarGridSpec(
        num_scalar_prefetch=3,
        grid=(n_row,),
        in_specs=in_specs,
        out_specs=pl.BlockSpec(out_shape, lambda r, lids, rids, rot: (0, 0)),
    )
    stations = n_row * n_chip
    flops = 2 * stations * slots * slots * rows * width * width
    return pl.pallas_call(
        functools.partial(gram_kernel, slots, rows, width, n_chip, carry_in),
        grid_spec=grid_spec,
        out_shape=jax.ShapeDtypeStruct(out_shape, jnp.float32),
        input_output_aliases={3: 0} if carry_in else {},
        compiler_params=pltpu.CompilerParams(
            dimension_semantics=("arbitrary",), vmem_limit_bytes=56 * 1024 * 1024
        ),
        cost_estimate=pl.CostEstimate(
            flops=flops,
            bytes_accessed=2 * right.size * 2 + per_row * per_col * width * width * 4,
            transcendentals=0,
        ),
    )(left_ids.reshape(-1), right_ids.reshape(-1), rot, *operands)

def shift(x, axis, step):
    n = lax.axis_size(axis)
    return lax.ppermute(x, axis, [(i, (i + step) % n) for i in range(n)])


def z_ring(piece):
    from_above = shift(piece, "z", -1)
    from_below = shift(piece, "z", 1)
    half = piece.shape[0] // 2
    far_low = shift(from_below[:half], "z", 1)
    far_high = shift(from_above[half:], "z", -1)
    far = jnp.concatenate([far_low, far_high], axis=0)
    return jnp.stack([piece, from_above, far, from_below])


def ring_gather(piece):
    other = shift(piece, "xlo", 1)
    first = lax.axis_index("xlo") == 0
    bundle = jnp.where(first, jnp.stack([piece, other]), jnp.stack([other, piece]))
    from_below = shift(bundle, "y", 1)
    from_above = shift(bundle, "y", -1)
    far_low = shift(from_below[:1], "y", 1)
    far_high = shift(from_above[1:], "y", -1)
    far = jnp.concatenate([far_low, far_high], axis=0)
    return jnp.stack([bundle, from_above, far, from_below])


def local(sensitivity, tile_ids, counts, weight_class):
    row_devices = lax.axis_size("xlo") * lax.axis_size("y")
    chips = lax.axis_size("xhi") * lax.axis_size("z")
    cores = lax.axis_size("core")
    me_core = lax.axis_index("core")
    blocks, owners, slots, rows, width = sensitivity.shape
    per_row = TILES // row_devices
    per_col = per_row // cores
    live = jnp.arange(slots, dtype=jnp.int32)[None, None, :] < counts[:, :, None]
    factor = station_scale(weight_class)[:, None, None, :, None] * live[:, :, :, None, None].astype(
        jnp.float32
    )
    weighted = (sensitivity.astype(jnp.float32) * factor).astype(jnp.bfloat16)
    live_ids = jnp.where(live, tile_ids, -1).astype(jnp.bfloat16)
    band = jnp.zeros((blocks, owners, slots, BAND, width), jnp.bfloat16)
    band = band.at[:, :, :, 0, :].set(live_ids[..., None])
    tagged = jnp.concatenate([weighted, band], axis=3)
    band_rows = rows + BAND

    left = lax.all_to_all(tagged, ("xlo", "y"), split_axis=1, concat_axis=0, tiled=True)
    left = z_ring(left[:, 0])
    left_own = jnp.stack([left, shift(left, "xhi", 1)])
    right = lax.all_to_all(tagged, ("xhi", "z"), split_axis=1, concat_axis=1, tiled=True)
    right_own = ring_gather(right[0])
    left_other = shift(left_own, "core", 1)
    right_other = shift(right_own, "core", 1)

    n_y = lax.axis_size("y")
    n_z = lax.axis_size("z")
    n_xhi = lax.axis_size("xhi")
    me_y = lax.axis_index("y")
    me_z = lax.axis_index("z")
    me_xhi = lax.axis_index("xhi")
    absolute_y = (jnp.arange(n_y, dtype=jnp.int32) - me_y) % n_y
    k_rel = jnp.arange(n_xhi * n_z, dtype=jnp.int32)
    chip_of = ((me_xhi + k_rel // n_z) % n_xhi) * n_z + (me_z + k_rel % n_z) % n_z

    def part(prev, left_half, right_half):
        left_ids = left_half[:, :, :, :, rows, 0].astype(jnp.int32)
        left_ids = jnp.transpose(left_ids, (2, 0, 1, 3))
        right_ids = right_half[:, :, :, :, rows, 0].astype(jnp.int32) - me_core * per_col
        right_ids = jnp.transpose(right_ids[absolute_y], (1, 0, 2, 3)).reshape(row_devices, chips, slots)
        right_ids = right_ids[:, chip_of]
        right_ids = jnp.where((right_ids >= 0) & (right_ids < per_col), right_ids, -1)
        rot = jnp.stack([me_y, me_xhi, me_z]).astype(jnp.int32)
        return accumulate(prev, left_half, left_ids, right_half, right_ids, rot, rows, per_row, per_col)

    normal = part(None, left_own, right_own)
    return part(normal, left_other, right_other)

def solution(mesh):
    row_devices, col_devices = mesh.devices.shape
    cores = 2
    x_lo = 2
    x_hi = 2
    mesh3 = jax.sharding.Mesh(
        mesh.devices.reshape(x_lo, row_devices // x_lo, x_hi, col_devices // cores // x_hi, cores),
        ("xlo", "y", "xhi", "z", "core"),
    )
    blocks = ("xlo", "y", "xhi", "z", "core")
    in_specs = (
        P(blocks, None, None, None, None),
        P(blocks, None, None),
        P(blocks, None),
        P(blocks, None),
    )
    out_specs = P(("xlo", "y"), ("xhi", "z", "core"))
    return jax.shard_map(local, mesh=mesh3, in_specs=in_specs, out_specs=out_specs, check_vma=False)
```

```python
import functools

import jax
import jax.numpy as jnp
from jax import lax
from jax.experimental import pallas as pl
from jax.experimental.pallas import tpu as pltpu
from jax.sharding import PartitionSpec as P

TILES = 128
BAND = 16


def station_scale(weight_class):
    levels = jnp.array([1.0, 0.5, 0.25, 0.125], jnp.float32)
    hits = weight_class[..., None] == jnp.arange(4, dtype=jnp.int32)
    return jnp.sum(jnp.where(hits, levels, jnp.float32(0.0)), axis=-1)


def gram_kernel(slots, rows, width, group, carry_in, lids_ref, rids_ref, rot_ref, *refs):
    if carry_in:
        prev_ref, left_ref, right_ref, out_ref = refs
    else:
        left_ref, right_ref, out_ref = refs
    r = pl.program_id(0)

    @pl.when(r == 0)
    def _():
        if carry_in:
            out_ref[...] = prev_ref[...]
        else:
            out_ref[...] = jnp.zeros_like(out_ref)

    n_z = left_ref.shape[0]
    n_xhi = left_ref.shape[1]

    def body(k, carry):
        b = r * group + k
        z_rel = k // n_xhi
        x_abs = lax.rem(k, n_xhi)
        chip = x_abs * n_z + lax.rem(rot_ref[2] + z_rel, n_z)
        for i in range(slots):
            li = lids_ref[b * slots + i]
            for j in range(slots):
                rj = rids_ref[b * slots + j]

                @pl.when((li >= 0) & (rj >= 0))
                def _():
                    prod = lax.dot_general(
                        left_ref[z_rel, x_abs, i, :rows, :],
                        right_ref[chip, j, :rows, :],
                        (((0,), (0,)), ((), ())),
                        preferred_element_type=jnp.float32,
                    )
                    out_rows = pl.ds(pl.multiple_of(li * width, width), width)
                    out_cols = pl.ds(pl.multiple_of(rj * width, width), width)
                    out_ref[out_rows, out_cols] += prod

        return carry

    lax.fori_loop(0, group, body, 0)


def accumulate(prev, left, left_ids, right, right_ids, rot, rows, per_row, per_col):
    n_z, n_row, n_xhi, slots, band_rows, width = left.shape
    n_chip = n_xhi * n_z
    n_y = right.shape[0]
    out_shape = (per_row * width, per_col * width)

    def right_map(r, lids, rids, rot):
        return (lax.rem(lax.rem(r, n_y) - rot[0] + n_y, n_y), r // n_y, 0, 0, 0, 0)

    in_specs = [
        pl.BlockSpec((n_z, None, n_xhi, slots, band_rows, width), lambda r, lids, rids, rot: (0, r, 0, 0, 0, 0)),
        pl.BlockSpec((None, None, n_chip, slots, band_rows, width), right_map),
    ]
    operands = [left, right]
    carry_in = prev is not None
    if carry_in:
        in_specs = [pl.BlockSpec(out_shape, lambda r, lids, rids, rot: (0, 0))] + in_specs
        operands = [prev] + operands
    grid_spec = pltpu.PrefetchScalarGridSpec(
        num_scalar_prefetch=3,
        grid=(n_row,),
        in_specs=in_specs,
        out_specs=pl.BlockSpec(out_shape, lambda r, lids, rids, rot: (0, 0)),
    )
    stations = n_row * n_chip
    flops = 2 * stations * slots * slots * rows * width * width
    return pl.pallas_call(
        functools.partial(gram_kernel, slots, rows, width, n_chip, carry_in),
        grid_spec=grid_spec,
        out_shape=jax.ShapeDtypeStruct(out_shape, jnp.float32),
        input_output_aliases={3: 0} if carry_in else {},
        compiler_params=pltpu.CompilerParams(
            dimension_semantics=("arbitrary",), vmem_limit_bytes=56 * 1024 * 1024
        ),
        cost_estimate=pl.CostEstimate(
            flops=flops,
            bytes_accessed=2 * right.size * 2 + per_row * per_col * width * width * 4,
            transcendentals=0,
        ),
    )(left_ids.reshape(-1), right_ids.reshape(-1), rot, *operands)

def shift(x, axis, step):
    n = lax.axis_size(axis)
    return lax.ppermute(x, axis, [(i, (i + step) % n) for i in range(n)])


def z_ring(piece):
    from_above = shift(piece, "z", -1)
    from_below = shift(piece, "z", 1)
    half = piece.shape[0] // 2
    far_low = shift(from_below[:half], "z", 1)
    far_high = shift(from_above[half:], "z", -1)
    far = jnp.concatenate([far_low, far_high], axis=0)
    return jnp.stack([piece, from_above, far, from_below])


def ring_gather(piece):
    other = shift(piece, "xlo", 1)
    first = lax.axis_index("xlo") == 0
    bundle = jnp.where(first, jnp.stack([piece, other]), jnp.stack([other, piece]))
    from_below = shift(bundle, "y", 1)
    from_above = shift(bundle, "y", -1)
    far_low = shift(from_below[:1], "y", 1)
    far_high = shift(from_above[1:], "y", -1)
    far = jnp.concatenate([far_low, far_high], axis=0)
    return jnp.stack([bundle, from_above, far, from_below])


def local(sensitivity, tile_ids, counts, weight_class):
    row_devices = lax.axis_size("xlo") * lax.axis_size("y")
    chips = lax.axis_size("xhi") * lax.axis_size("z")
    cores = lax.axis_size("core")
    me_core = lax.axis_index("core")
    blocks, owners, slots, rows, width = sensitivity.shape
    per_row = TILES // row_devices
    per_col = per_row // cores
    live = jnp.arange(slots, dtype=jnp.int32)[None, None, :] < counts[:, :, None]
    factor = station_scale(weight_class)[:, None, None, :, None] * live[:, :, :, None, None].astype(
        jnp.float32
    )
    weighted = (sensitivity.astype(jnp.float32) * factor).astype(jnp.bfloat16)
    live_ids = jnp.where(live, tile_ids, -1).astype(jnp.bfloat16)
    band = jnp.zeros((blocks, owners, slots, BAND, width), jnp.bfloat16)
    band = band.at[:, :, :, 0, :].set(live_ids[..., None])
    tagged = jnp.concatenate([weighted, band], axis=3)
    band_rows = rows + BAND

    left = lax.all_to_all(tagged, ("xlo", "y"), split_axis=1, concat_axis=0, tiled=True)
    left = left[:, 0]
    first = lax.axis_index("xhi") == 0
    other = shift(left, "xhi", 1)
    left = jnp.where(first, jnp.stack([left, other], axis=1), jnp.stack([other, left], axis=1))
    left_own = z_ring(left)
    right = lax.all_to_all(tagged, ("xhi", "z"), split_axis=1, concat_axis=1, tiled=True)
    right_own = ring_gather(right[0])
    left_other = shift(left_own, "core", 1)
    right_other = shift(right_own, "core", 1)

    n_y = lax.axis_size("y")
    n_z = lax.axis_size("z")
    n_xhi = lax.axis_size("xhi")
    me_y = lax.axis_index("y")
    me_z = lax.axis_index("z")
    me_xhi = lax.axis_index("xhi")
    absolute_y = (jnp.arange(n_y, dtype=jnp.int32) - me_y) % n_y
    k_rel = jnp.arange(n_xhi * n_z, dtype=jnp.int32)
    chip_of = (k_rel % n_xhi) * n_z + (me_z + k_rel // n_xhi) % n_z

    def part(prev, left_half, right_half):
        left_ids = left_half[:, :, :, :, rows, 0].astype(jnp.int32)
        left_ids = jnp.transpose(left_ids, (1, 0, 2, 3))
        right_ids = right_half[:, :, :, :, rows, 0].astype(jnp.int32) - me_core * per_col
        right_ids = jnp.transpose(right_ids[absolute_y], (1, 0, 2, 3)).reshape(row_devices, chips, slots)
        right_ids = right_ids[:, chip_of]
        right_ids = jnp.where((right_ids >= 0) & (right_ids < per_col), right_ids, -1)
        rot = jnp.stack([me_y, me_xhi, me_z]).astype(jnp.int32)
        return accumulate(prev, left_half, left_ids, right_half, right_ids, rot, rows, per_row, per_col)

    normal = part(None, left_own, right_own)
    return part(normal, left_other, right_other)

def solution(mesh):
    row_devices, col_devices = mesh.devices.shape
    cores = 2
    x_lo = 2
    x_hi = 2
    mesh3 = jax.sharding.Mesh(
        mesh.devices.reshape(x_lo, row_devices // x_lo, x_hi, col_devices // cores // x_hi, cores),
        ("xlo", "y", "xhi", "z", "core"),
    )
    blocks = ("xlo", "y", "xhi", "z", "core")
    in_specs = (
        P(blocks, None, None, None, None),
        P(blocks, None, None),
        P(blocks, None),
        P(blocks, None),
    )
    out_specs = P(("xlo", "y"), ("xhi", "z", "core"))
    return jax.shard_map(local, mesh=mesh3, in_specs=in_specs, out_specs=out_specs, check_vma=False)
```

```python
import functools

import jax
import jax.numpy as jnp
from jax import lax
from jax.experimental import pallas as pl
from jax.experimental.pallas import tpu as pltpu
from jax.sharding import PartitionSpec as P

TILES = 128
BAND = 16


def station_scale(weight_class):
    levels = jnp.array([1.0, 0.5, 0.25, 0.125], jnp.float32)
    hits = weight_class[..., None] == jnp.arange(4, dtype=jnp.int32)
    return jnp.sum(jnp.where(hits, levels, jnp.float32(0.0)), axis=-1)


def gram_kernel(slots, rows, width, group, carry_in, lids_ref, rids_ref, rot_ref, *refs):
    if carry_in:
        prev_ref, left_ref, right_ref, out_ref = refs
    else:
        left_ref, right_ref, out_ref = refs
    r = pl.program_id(0)

    @pl.when(r == 0)
    def _():
        if carry_in:
            out_ref[...] = prev_ref[...]
        else:
            out_ref[...] = jnp.zeros_like(out_ref)

    n_z = left_ref.shape[0]
    n_xhi = left_ref.shape[1]

    def body(k, carry):
        b = r * group + k
        z_rel = k // n_xhi
        x_abs = lax.rem(k, n_xhi)
        chip = x_abs * n_z + lax.rem(rot_ref[2] + z_rel, n_z)
        lids = [lids_ref[b * slots + i] for i in range(slots)]
        rids = [rids_ref[b * slots + j] for j in range(slots)]
        any_left = functools.reduce(jnp.logical_or, [li >= 0 for li in lids])
        any_right = functools.reduce(jnp.logical_or, [rj >= 0 for rj in rids])

        @pl.when(any_left & any_right)
        def _():
            lhs = jnp.concatenate([left_ref[z_rel, x_abs, i, :rows, :] for i in range(slots)], axis=1)
            rhs = jnp.concatenate([right_ref[chip, j, :rows, :] for j in range(slots)], axis=1)
            gram = lax.dot_general(
                lhs, rhs, (((0,), (0,)), ((), ())), preferred_element_type=jnp.float32
            )
            for i in range(slots):
                for j in range(slots):

                    @pl.when((lids[i] >= 0) & (rids[j] >= 0))
                    def _():
                        out_rows = pl.ds(pl.multiple_of(lids[i] * width, width), width)
                        out_cols = pl.ds(pl.multiple_of(rids[j] * width, width), width)
                        out_ref[out_rows, out_cols] += gram[i * width:(i + 1) * width, j * width:(j + 1) * width]

        return carry

    lax.fori_loop(0, group, body, 0)


def accumulate(prev, left, left_ids, right, right_ids, rot, rows, per_row, per_col):
    n_z, n_row, n_xhi, slots, band_rows, width = left.shape
    n_chip = n_xhi * n_z
    n_y = right.shape[0]
    out_shape = (per_row * width, per_col * width)

    def right_map(r, lids, rids, rot):
        return (lax.rem(lax.rem(r, n_y) - rot[0] + n_y, n_y), r // n_y, 0, 0, 0, 0)

    in_specs = [
        pl.BlockSpec((n_z, None, n_xhi, slots, band_rows, width), lambda r, lids, rids, rot: (0, r, 0, 0, 0, 0)),
        pl.BlockSpec((None, None, n_chip, slots, band_rows, width), right_map),
    ]
    operands = [left, right]
    carry_in = prev is not None
    if carry_in:
        in_specs = [pl.BlockSpec(out_shape, lambda r, lids, rids, rot: (0, 0))] + in_specs
        operands = [prev] + operands
    grid_spec = pltpu.PrefetchScalarGridSpec(
        num_scalar_prefetch=3,
        grid=(n_row,),
        in_specs=in_specs,
        out_specs=pl.BlockSpec(out_shape, lambda r, lids, rids, rot: (0, 0)),
    )
    stations = n_row * n_chip
    flops = 2 * stations * slots * slots * rows * width * width
    return pl.pallas_call(
        functools.partial(gram_kernel, slots, rows, width, n_chip, carry_in),
        grid_spec=grid_spec,
        out_shape=jax.ShapeDtypeStruct(out_shape, jnp.float32),
        input_output_aliases={3: 0} if carry_in else {},
        compiler_params=pltpu.CompilerParams(
            dimension_semantics=("arbitrary",), vmem_limit_bytes=56 * 1024 * 1024
        ),
        cost_estimate=pl.CostEstimate(
            flops=flops,
            bytes_accessed=2 * right.size * 2 + per_row * per_col * width * width * 4,
            transcendentals=0,
        ),
    )(left_ids.reshape(-1), right_ids.reshape(-1), rot, *operands)

def shift(x, axis, step):
    n = lax.axis_size(axis)
    return lax.ppermute(x, axis, [(i, (i + step) % n) for i in range(n)])


def z_ring(piece):
    from_above = shift(piece, "z", -1)
    from_below = shift(piece, "z", 1)
    half = piece.shape[0] // 2
    far_low = shift(from_below[:half], "z", 1)
    far_high = shift(from_above[half:], "z", -1)
    far = jnp.concatenate([far_low, far_high], axis=0)
    return jnp.stack([piece, from_above, far, from_below])


def ring_gather(piece):
    other = shift(piece, "xlo", 1)
    first = lax.axis_index("xlo") == 0
    bundle = jnp.where(first, jnp.stack([piece, other]), jnp.stack([other, piece]))
    from_below = shift(bundle, "y", 1)
    from_above = shift(bundle, "y", -1)
    far_low = shift(from_below[:1], "y", 1)
    far_high = shift(from_above[1:], "y", -1)
    far = jnp.concatenate([far_low, far_high], axis=0)
    return jnp.stack([bundle, from_above, far, from_below])


def local(sensitivity, tile_ids, counts, weight_class):
    row_devices = lax.axis_size("xlo") * lax.axis_size("y")
    chips = lax.axis_size("xhi") * lax.axis_size("z")
    cores = lax.axis_size("core")
    me_core = lax.axis_index("core")
    blocks, owners, slots, rows, width = sensitivity.shape
    per_row = TILES // row_devices
    per_col = per_row // cores
    live = jnp.arange(slots, dtype=jnp.int32)[None, None, :] < counts[:, :, None]
    factor = station_scale(weight_class)[:, None, None, :, None] * live[:, :, :, None, None].astype(
        jnp.float32
    )
    weighted = (sensitivity.astype(jnp.float32) * factor).astype(jnp.bfloat16)
    live_ids = jnp.where(live, tile_ids, -1).astype(jnp.bfloat16)
    band = jnp.zeros((blocks, owners, slots, BAND, width), jnp.bfloat16)
    band = band.at[:, :, :, 0, :].set(live_ids[..., None])
    tagged = jnp.concatenate([weighted, band], axis=3)
    band_rows = rows + BAND

    left = lax.all_to_all(tagged, ("xlo", "y"), split_axis=1, concat_axis=0, tiled=True)
    left = left[:, 0]
    first = lax.axis_index("xhi") == 0
    other = shift(left, "xhi", 1)
    left = jnp.where(first, jnp.stack([left, other], axis=1), jnp.stack([other, left], axis=1))
    left_own = z_ring(left)
    right = lax.all_to_all(tagged, ("xhi", "z"), split_axis=1, concat_axis=1, tiled=True)
    right_own = ring_gather(right[0])
    left_other = shift(left_own, "core", 1)
    right_other = shift(right_own, "core", 1)

    n_y = lax.axis_size("y")
    n_z = lax.axis_size("z")
    n_xhi = lax.axis_size("xhi")
    me_y = lax.axis_index("y")
    me_z = lax.axis_index("z")
    me_xhi = lax.axis_index("xhi")
    absolute_y = (jnp.arange(n_y, dtype=jnp.int32) - me_y) % n_y
    k_rel = jnp.arange(n_xhi * n_z, dtype=jnp.int32)
    chip_of = (k_rel % n_xhi) * n_z + (me_z + k_rel // n_xhi) % n_z

    def part(prev, left_half, right_half):
        left_ids = left_half[:, :, :, :, rows, 0].astype(jnp.int32)
        left_ids = jnp.transpose(left_ids, (1, 0, 2, 3))
        right_ids = right_half[:, :, :, :, rows, 0].astype(jnp.int32) - me_core * per_col
        right_ids = jnp.transpose(right_ids[absolute_y], (1, 0, 2, 3)).reshape(row_devices, chips, slots)
        right_ids = right_ids[:, chip_of]
        right_ids = jnp.where((right_ids >= 0) & (right_ids < per_col), right_ids, -1)
        rot = jnp.stack([me_y, me_xhi, me_z]).astype(jnp.int32)
        return accumulate(prev, left_half, left_ids, right_half, right_ids, rot, rows, per_row, per_col)

    normal = part(None, left_own, right_own)
    return part(normal, left_other, right_other)

def solution(mesh):
    row_devices, col_devices = mesh.devices.shape
    cores = 2
    x_lo = 2
    x_hi = 2
    mesh3 = jax.sharding.Mesh(
        mesh.devices.reshape(x_lo, row_devices // x_lo, x_hi, col_devices // cores // x_hi, cores),
        ("xlo", "y", "xhi", "z", "core"),
    )
    blocks = ("xlo", "y", "xhi", "z", "core")
    in_specs = (
        P(blocks, None, None, None, None),
        P(blocks, None, None),
        P(blocks, None),
        P(blocks, None),
    )
    out_specs = P(("xlo", "y"), ("xhi", "z", "core"))
    return jax.shard_map(local, mesh=mesh3, in_specs=in_specs, out_specs=out_specs, check_vma=False)
```

```python
import functools

import jax
import jax.numpy as jnp
from jax import lax
from jax.experimental import pallas as pl
from jax.experimental.pallas import tpu as pltpu
from jax.sharding import PartitionSpec as P

TILES = 128
BAND = 16


def station_scale(weight_class):
    levels = jnp.array([1.0, 0.5, 0.25, 0.125], jnp.float32)
    hits = weight_class[..., None] == jnp.arange(4, dtype=jnp.int32)
    return jnp.sum(jnp.where(hits, levels, jnp.float32(0.0)), axis=-1)


def gram_kernel(slots, rows, width, group, carry_in, lids_ref, rids_ref, rot_ref, *refs):
    if carry_in:
        prev_ref, left_ref, right_ref, out_ref = refs
    else:
        left_ref, right_ref, out_ref = refs
    r = pl.program_id(0)

    @pl.when(r == 0)
    def _():
        if carry_in:
            out_ref[...] = prev_ref[...]
        else:
            out_ref[...] = jnp.zeros_like(out_ref)

    n_xhi = left_ref.shape[1]
    n_chip_z = right_ref.shape[0] // n_xhi

    def body(k, carry):
        b = r * group + k
        piece = k // n_xhi
        x_abs = lax.rem(k, n_xhi)
        chip = x_abs * n_chip_z + lax.rem(rot_ref[2] + rot_ref[3 + piece], n_chip_z)
        lids = [lids_ref[b * slots + i] for i in range(slots)]
        rids = [rids_ref[b * slots + j] for j in range(slots)]
        any_left = functools.reduce(jnp.logical_or, [li >= 0 for li in lids])
        any_right = functools.reduce(jnp.logical_or, [rj >= 0 for rj in rids])

        @pl.when(any_left & any_right)
        def _():
            lhs = jnp.concatenate([left_ref[piece, x_abs, i, :rows, :] for i in range(slots)], axis=1)
            rhs = jnp.concatenate([right_ref[chip, j, :rows, :] for j in range(slots)], axis=1)
            gram = lax.dot_general(
                lhs, rhs, (((0,), (0,)), ((), ())), preferred_element_type=jnp.float32
            )
            for i in range(slots):
                for j in range(slots):

                    @pl.when((lids[i] >= 0) & (rids[j] >= 0))
                    def _():
                        out_rows = pl.ds(pl.multiple_of(lids[i] * width, width), width)
                        out_cols = pl.ds(pl.multiple_of(rids[j] * width, width), width)
                        out_ref[out_rows, out_cols] += gram[i * width:(i + 1) * width, j * width:(j + 1) * width]

        return carry

    lax.fori_loop(0, group, body, 0)


def accumulate(prev, left, left_ids, right, right_ids, rot, rows, per_row, per_col):
    n_piece, n_row, n_xhi, slots, band_rows, width = left.shape
    n_chip = n_xhi * n_piece
    n_y = right.shape[0]
    out_shape = (per_row * width, per_col * width)

    def right_map(r, lids, rids, rot):
        return (lax.rem(lax.rem(r, n_y) - rot[0] + n_y, n_y), r // n_y, 0, 0, 0, 0)

    in_specs = [
        pl.BlockSpec((n_piece, None, n_xhi, slots, band_rows, width), lambda r, lids, rids, rot: (0, r, 0, 0, 0, 0)),
        pl.BlockSpec((None, None, right.shape[2], slots, band_rows, width), right_map),
    ]
    operands = [left, right]
    carry_in = prev is not None
    if carry_in:
        in_specs = [pl.BlockSpec(out_shape, lambda r, lids, rids, rot: (0, 0))] + in_specs
        operands = [prev] + operands
    grid_spec = pltpu.PrefetchScalarGridSpec(
        num_scalar_prefetch=3,
        grid=(n_row,),
        in_specs=in_specs,
        out_specs=pl.BlockSpec(out_shape, lambda r, lids, rids, rot: (0, 0)),
    )
    stations = n_row * n_chip
    flops = 2 * stations * slots * slots * rows * width * width
    return pl.pallas_call(
        functools.partial(gram_kernel, slots, rows, width, n_chip, carry_in),
        grid_spec=grid_spec,
        out_shape=jax.ShapeDtypeStruct(out_shape, jnp.float32),
        input_output_aliases={3: 0} if carry_in else {},
        compiler_params=pltpu.CompilerParams(
            dimension_semantics=("arbitrary",), vmem_limit_bytes=56 * 1024 * 1024
        ),
        cost_estimate=pl.CostEstimate(
            flops=flops,
            bytes_accessed=2 * right.size * 2 + per_row * per_col * width * width * 4,
            transcendentals=0,
        ),
    )(left_ids.reshape(-1), right_ids.reshape(-1), rot, *operands)

def shift(x, axis, step):
    n = lax.axis_size(axis)
    return lax.ppermute(x, axis, [(i, (i + step) % n) for i in range(n)])


def z_ring(piece):
    from_above = shift(piece, "z", -1)
    from_below = shift(piece, "z", 1)
    half = piece.shape[0] // 2
    far_low = shift(from_below[:half], "z", 1)
    far_high = shift(from_above[half:], "z", -1)
    far = jnp.concatenate([far_low, far_high], axis=0)
    return jnp.stack([piece, from_above, from_below]), far[None]


def ring_gather(piece):
    other = shift(piece, "xlo", 1)
    first = lax.axis_index("xlo") == 0
    bundle = jnp.where(first, jnp.stack([piece, other]), jnp.stack([other, piece]))
    from_below = shift(bundle, "y", 1)
    from_above = shift(bundle, "y", -1)
    far_low = shift(from_below[:1], "y", 1)
    far_high = shift(from_above[1:], "y", -1)
    far = jnp.concatenate([far_low, far_high], axis=0)
    return jnp.stack([bundle, from_above, far, from_below])


def local(sensitivity, tile_ids, counts, weight_class):
    row_devices = lax.axis_size("xlo") * lax.axis_size("y")
    chips = lax.axis_size("xhi") * lax.axis_size("z")
    cores = lax.axis_size("core")
    me_core = lax.axis_index("core")
    blocks, owners, slots, rows, width = sensitivity.shape
    per_row = TILES // row_devices
    per_col = per_row // cores
    live = jnp.arange(slots, dtype=jnp.int32)[None, None, :] < counts[:, :, None]
    factor = station_scale(weight_class)[:, None, None, :, None] * live[:, :, :, None, None].astype(
        jnp.float32
    )
    weighted = (sensitivity.astype(jnp.float32) * factor).astype(jnp.bfloat16)
    live_ids = jnp.where(live, tile_ids, -1).astype(jnp.bfloat16)
    band = jnp.zeros((blocks, owners, slots, BAND, width), jnp.bfloat16)
    band = band.at[:, :, :, 0, :].set(live_ids[..., None])
    tagged = jnp.concatenate([weighted, band], axis=3)
    band_rows = rows + BAND

    left = lax.all_to_all(tagged, ("xlo", "y"), split_axis=1, concat_axis=0, tiled=True)
    left = left[:, 0]
    first = lax.axis_index("xhi") == 0
    other = shift(left, "xhi", 1)
    left = jnp.where(first, jnp.stack([left, other], axis=1), jnp.stack([other, left], axis=1))
    near_own, far_own = z_ring(left)
    right = lax.all_to_all(tagged, ("xhi", "z"), split_axis=1, concat_axis=1, tiled=True)
    right_own = ring_gather(right[0])
    near_other = shift(near_own, "core", 1)
    far_other = shift(far_own, "core", 1)
    right_other = shift(right_own, "core", 1)

    n_y = lax.axis_size("y")
    n_z = lax.axis_size("z")
    n_xhi = lax.axis_size("xhi")
    me_y = lax.axis_index("y")
    me_z = lax.axis_index("z")
    me_xhi = lax.axis_index("xhi")
    absolute_y = (jnp.arange(n_y, dtype=jnp.int32) - me_y) % n_y

    def part(prev, left_half, steps, right_half):
        n_piece = len(steps)
        left_ids = left_half[:, :, :, :, rows, 0].astype(jnp.int32)
        left_ids = jnp.transpose(left_ids, (1, 0, 2, 3))
        right_ids = right_half[:, :, :, :, rows, 0].astype(jnp.int32) - me_core * per_col
        right_ids = jnp.transpose(right_ids[absolute_y], (1, 0, 2, 3)).reshape(row_devices, chips, slots)
        k_rel = jnp.arange(n_xhi * n_piece, dtype=jnp.int32)
        z_step = jnp.array(steps, jnp.int32)[k_rel // n_xhi]
        chip_of = (k_rel % n_xhi) * n_z + (me_z + z_step) % n_z
        right_ids = right_ids[:, chip_of]
        right_ids = jnp.where((right_ids >= 0) & (right_ids < per_col), right_ids, -1)
        rot = jnp.concatenate([jnp.stack([me_y, me_xhi, me_z]), jnp.array(steps)]).astype(jnp.int32)
        return accumulate(prev, left_half, left_ids, right_half, right_ids, rot, rows, per_row, per_col)

    near_steps = (0, 1, n_z - 1)
    far_steps = (2,)
    normal = part(None, near_own, near_steps, right_own)
    normal = part(normal, far_own, far_steps, right_own)
    normal = part(normal, near_other, near_steps, right_other)
    return part(normal, far_other, far_steps, right_other)

def solution(mesh):
    row_devices, col_devices = mesh.devices.shape
    cores = 2
    x_lo = 2
    x_hi = 2
    mesh3 = jax.sharding.Mesh(
        mesh.devices.reshape(x_lo, row_devices // x_lo, x_hi, col_devices // cores // x_hi, cores),
        ("xlo", "y", "xhi", "z", "core"),
    )
    blocks = ("xlo", "y", "xhi", "z", "core")
    in_specs = (
        P(blocks, None, None, None, None),
        P(blocks, None, None),
        P(blocks, None),
        P(blocks, None),
    )
    out_specs = P(("xlo", "y"), ("xhi", "z", "core"))
    return jax.shard_map(local, mesh=mesh3, in_specs=in_specs, out_specs=out_specs, check_vma=False)
```

```python
import functools

import jax
import jax.numpy as jnp
from jax import lax
from jax.experimental import pallas as pl
from jax.experimental.pallas import tpu as pltpu
from jax.sharding import PartitionSpec as P

TILES = 128
BAND = 16


def station_scale(weight_class):
    levels = jnp.array([1.0, 0.5, 0.25, 0.125], jnp.float32)
    hits = weight_class[..., None] == jnp.arange(4, dtype=jnp.int32)
    return jnp.sum(jnp.where(hits, levels, jnp.float32(0.0)), axis=-1)


def gram_kernel(slots, rows, width, group, carry_in, lids_ref, rids_ref, rot_ref, *refs):
    if carry_in:
        prev_ref, left_ref, right_ref, out_ref = refs
    else:
        left_ref, right_ref, out_ref = refs
    r = pl.program_id(0)

    @pl.when(r == 0)
    def _():
        if carry_in:
            out_ref[...] = prev_ref[...]
        else:
            out_ref[...] = jnp.zeros_like(out_ref)

    n_z = left_ref.shape[0]
    n_xhi = left_ref.shape[1]

    def body(k, carry):
        b = r * group + k
        z_rel = k // n_xhi
        x_abs = lax.rem(k, n_xhi)
        chip = x_abs * n_z + lax.rem(rot_ref[2] + z_rel, n_z)
        lids = [lids_ref[b * slots + i] for i in range(slots)]
        rids = [rids_ref[b * slots + j] for j in range(slots)]
        any_left = functools.reduce(jnp.logical_or, [li >= 0 for li in lids])
        any_right = functools.reduce(jnp.logical_or, [rj >= 0 for rj in rids])

        @pl.when(any_left & any_right)
        def _():
            lhs = jnp.concatenate([left_ref[z_rel, x_abs, i, :rows, :] for i in range(slots)], axis=1)
            rhs = jnp.concatenate([right_ref[chip, j, :rows, :] for j in range(slots)], axis=1)
            gram = lax.dot_general(
                lhs, rhs, (((0,), (0,)), ((), ())), preferred_element_type=jnp.float32
            )
            for i in range(slots):
                for j in range(slots):

                    @pl.when((lids[i] >= 0) & (rids[j] >= 0))
                    def _():
                        out_rows = pl.ds(pl.multiple_of(lids[i] * width, width), width)
                        out_cols = pl.ds(pl.multiple_of(rids[j] * width, width), width)
                        out_ref[out_rows, out_cols] += gram[i * width:(i + 1) * width, j * width:(j + 1) * width]

        return carry

    lax.fori_loop(0, group, body, 0)


def accumulate(prev, left, left_ids, right, right_ids, rot, rows, per_row, per_col):
    n_z, n_row, n_xhi, slots, band_rows, width = left.shape
    n_chip = n_xhi * n_z
    n_y = right.shape[0]
    out_shape = (per_row * width, per_col * width)

    def right_map(r, lids, rids, rot):
        return (lax.rem(lax.rem(r, n_y) - rot[0] + n_y, n_y), r // n_y, 0, 0, 0, 0)

    in_specs = [
        pl.BlockSpec((n_z, None, n_xhi, slots, band_rows, width), lambda r, lids, rids, rot: (0, r, 0, 0, 0, 0)),
        pl.BlockSpec((None, None, n_chip, slots, band_rows, width), right_map),
    ]
    operands = [left, right]
    carry_in = prev is not None
    if carry_in:
        in_specs = [pl.BlockSpec(out_shape, lambda r, lids, rids, rot: (0, 0))] + in_specs
        operands = [prev] + operands
    grid_spec = pltpu.PrefetchScalarGridSpec(
        num_scalar_prefetch=3,
        grid=(n_row,),
        in_specs=in_specs,
        out_specs=pl.BlockSpec(out_shape, lambda r, lids, rids, rot: (0, 0)),
    )
    stations = n_row * n_chip
    flops = 2 * stations * slots * slots * rows * width * width
    return pl.pallas_call(
        functools.partial(gram_kernel, slots, rows, width, n_chip, carry_in),
        grid_spec=grid_spec,
        out_shape=jax.ShapeDtypeStruct(out_shape, jnp.float32),
        input_output_aliases={3: 0} if carry_in else {},
        compiler_params=pltpu.CompilerParams(
            dimension_semantics=("arbitrary",), vmem_limit_bytes=56 * 1024 * 1024
        ),
        cost_estimate=pl.CostEstimate(
            flops=flops,
            bytes_accessed=2 * right.size * 2 + per_row * per_col * width * width * 4,
            transcendentals=0,
        ),
    )(left_ids.reshape(-1), right_ids.reshape(-1), rot, *operands)

def shift(x, axis, step):
    n = lax.axis_size(axis)
    return lax.ppermute(x, axis, [(i, (i + step) % n) for i in range(n)])


def z_ring(piece):
    from_above = shift(piece, "z", -1)
    from_below = shift(piece, "z", 1)
    half = piece.shape[0] // 2
    far_low = shift(from_below[:half], "z", 1)
    far_high = shift(from_above[half:], "z", -1)
    far = jnp.concatenate([far_low, far_high], axis=0)
    return jnp.stack([piece, from_above, far, from_below])


def ring_gather(bundle):
    from_below = shift(bundle, "y", 1)
    from_above = shift(bundle, "y", -1)
    far_low = shift(from_below[:1], "y", 1)
    far_high = shift(from_above[1:], "y", -1)
    far = jnp.concatenate([far_low, far_high], axis=0)
    return jnp.stack([bundle, from_above, far, from_below])


def local(sensitivity, tile_ids, counts, weight_class):
    row_devices = lax.axis_size("xlo") * lax.axis_size("y")
    chips = lax.axis_size("xhi") * lax.axis_size("z")
    cores = lax.axis_size("core")
    me_core = lax.axis_index("core")
    blocks, owners, slots, rows, width = sensitivity.shape
    per_row = TILES // row_devices
    per_col = per_row // cores
    live = jnp.arange(slots, dtype=jnp.int32)[None, None, :] < counts[:, :, None]
    factor = station_scale(weight_class)[:, None, None, :, None] * live[:, :, :, None, None].astype(
        jnp.float32
    )
    weighted = (sensitivity.astype(jnp.float32) * factor).astype(jnp.bfloat16)
    live_ids = jnp.where(live, tile_ids, -1).astype(jnp.bfloat16)
    band = jnp.zeros((blocks, owners, slots, BAND, width), jnp.bfloat16)
    band = band.at[:, :, :, 0, :].set(live_ids[..., None])
    tagged = jnp.concatenate([weighted, band], axis=3)
    band_rows = rows + BAND

    n_xhi = lax.axis_size("xhi")
    n_xlo = lax.axis_size("xlo")
    doubled = jnp.repeat(tagged, n_xhi, axis=1)
    left = lax.all_to_all(doubled, ("xlo", "y", "xhi"), split_axis=1, concat_axis=0, tiled=True)
    left = left.reshape(row_devices, n_xhi, slots, band_rows, width)
    left_own = z_ring(left)
    doubled = jnp.concatenate([tagged] * n_xlo, axis=1)
    right = lax.all_to_all(doubled, ("xlo", "xhi", "z"), split_axis=1, concat_axis=0, tiled=True)
    right_own = ring_gather(right.reshape(n_xlo, chips, slots, band_rows, width))
    left_other = shift(left_own, "core", 1)
    right_other = shift(right_own, "core", 1)

    n_y = lax.axis_size("y")
    n_z = lax.axis_size("z")
    me_y = lax.axis_index("y")
    me_z = lax.axis_index("z")
    me_xhi = lax.axis_index("xhi")
    absolute_y = (jnp.arange(n_y, dtype=jnp.int32) - me_y) % n_y
    k_rel = jnp.arange(n_xhi * n_z, dtype=jnp.int32)
    chip_of = (k_rel % n_xhi) * n_z + (me_z + k_rel // n_xhi) % n_z

    def part(prev, left_half, right_half):
        left_ids = left_half[:, :, :, :, rows, 0].astype(jnp.int32)
        left_ids = jnp.transpose(left_ids, (1, 0, 2, 3))
        right_ids = right_half[:, :, :, :, rows, 0].astype(jnp.int32) - me_core * per_col
        right_ids = jnp.transpose(right_ids[absolute_y], (1, 0, 2, 3)).reshape(row_devices, chips, slots)
        right_ids = right_ids[:, chip_of]
        right_ids = jnp.where((right_ids >= 0) & (right_ids < per_col), right_ids, -1)
        rot = jnp.stack([me_y, me_xhi, me_z]).astype(jnp.int32)
        return accumulate(prev, left_half, left_ids, right_half, right_ids, rot, rows, per_row, per_col)

    normal = part(None, left_own, right_own)
    return part(normal, left_other, right_other)

def solution(mesh):
    row_devices, col_devices = mesh.devices.shape
    cores = 2
    x_lo = 2
    x_hi = 2
    mesh3 = jax.sharding.Mesh(
        mesh.devices.reshape(x_lo, row_devices // x_lo, x_hi, col_devices // cores // x_hi, cores),
        ("xlo", "y", "xhi", "z", "core"),
    )
    blocks = ("xlo", "y", "xhi", "z", "core")
    in_specs = (
        P(blocks, None, None, None, None),
        P(blocks, None, None),
        P(blocks, None),
        P(blocks, None),
    )
    out_specs = P(("xlo", "y"), ("xhi", "z", "core"))
    return jax.shard_map(local, mesh=mesh3, in_specs=in_specs, out_specs=out_specs, check_vma=False)
```

```python
import functools

import jax
import jax.numpy as jnp
from jax import lax
from jax.experimental import pallas as pl
from jax.experimental.pallas import tpu as pltpu
from jax.sharding import PartitionSpec as P

TILES = 128
BAND = 16


def station_scale(weight_class):
    levels = jnp.array([1.0, 0.5, 0.25, 0.125], jnp.float32)
    hits = weight_class[..., None] == jnp.arange(4, dtype=jnp.int32)
    return jnp.sum(jnp.where(hits, levels, jnp.float32(0.0)), axis=-1)


def gram_kernel(slots, rows, width, group, lids_ref, rids_ref, rot_ref,
                left_own, right_own, left_other, right_other, out_ref):
    h = pl.program_id(0)
    r = pl.program_id(1)

    @pl.when((h == 0) & (r == 0))
    def _():
        out_ref[...] = jnp.zeros_like(out_ref)

    n_z = left_own.shape[0]
    n_xhi = left_own.shape[1]

    def run(left_ref, right_ref):
        def body(k, carry):
            b = (h * pl.num_programs(1) + r) * group + k
            z_rel = k // n_xhi
            x_abs = lax.rem(k, n_xhi)
            chip = x_abs * n_z + lax.rem(rot_ref[2] + z_rel, n_z)
            lids = [lids_ref[b * slots + i] for i in range(slots)]
            rids = [rids_ref[b * slots + j] for j in range(slots)]
            any_left = functools.reduce(jnp.logical_or, [li >= 0 for li in lids])
            any_right = functools.reduce(jnp.logical_or, [rj >= 0 for rj in rids])

            @pl.when(any_left & any_right)
            def _():
                lhs = jnp.concatenate([left_ref[z_rel, x_abs, i, :rows, :] for i in range(slots)], axis=1)
                rhs = jnp.concatenate([right_ref[chip, j, :rows, :] for j in range(slots)], axis=1)
                gram = lax.dot_general(
                    lhs, rhs, (((0,), (0,)), ((), ())), preferred_element_type=jnp.float32
                )
                for i in range(slots):
                    for j in range(slots):

                        @pl.when((lids[i] >= 0) & (rids[j] >= 0))
                        def _():
                            out_rows = pl.ds(pl.multiple_of(lids[i] * width, width), width)
                            out_cols = pl.ds(pl.multiple_of(rids[j] * width, width), width)
                            out_ref[out_rows, out_cols] += gram[i * width:(i + 1) * width, j * width:(j + 1) * width]

            return carry

        lax.fori_loop(0, group, body, 0)

    @pl.when(h == 0)
    def _():
        run(left_own, right_own)

    @pl.when(h == 1)
    def _():
        run(left_other, right_other)


def accumulate(left_own, right_own, left_other, right_other, left_ids, right_ids, rot, rows, per_row, per_col):
    n_z, n_row, n_xhi, slots, band_rows, width = left_own.shape
    n_chip = n_xhi * n_z
    n_y = right_own.shape[0]
    last = n_row - 1
    out_shape = (per_row * width, per_col * width)

    def right_block(r, rot):
        return (lax.rem(lax.rem(r, n_y) - rot[0] + n_y, n_y), r // n_y, 0, 0, 0, 0)

    left_block = (n_z, None, n_xhi, slots, band_rows, width)
    right_spec = (None, None, n_chip, slots, band_rows, width)
    in_specs = [
        pl.BlockSpec(left_block, lambda h, r, lids, rids, rot: (0, jnp.where(h == 0, r, last), 0, 0, 0, 0)),
        pl.BlockSpec(right_spec, lambda h, r, lids, rids, rot: right_block(jnp.where(h == 0, r, last), rot)),
        pl.BlockSpec(left_block, lambda h, r, lids, rids, rot: (0, jnp.where(h == 0, 0, r), 0, 0, 0, 0)),
        pl.BlockSpec(right_spec, lambda h, r, lids, rids, rot: right_block(jnp.where(h == 0, 0, r), rot)),
    ]
    grid_spec = pltpu.PrefetchScalarGridSpec(
        num_scalar_prefetch=3,
        grid=(2, n_row),
        in_specs=in_specs,
        out_specs=pl.BlockSpec(out_shape, lambda h, r, lids, rids, rot: (0, 0)),
    )
    stations = 2 * n_row * n_chip
    flops = 2 * stations * slots * slots * rows * width * width
    return pl.pallas_call(
        functools.partial(gram_kernel, slots, rows, width, n_chip),
        grid_spec=grid_spec,
        out_shape=jax.ShapeDtypeStruct(out_shape, jnp.float32),
        compiler_params=pltpu.CompilerParams(
            dimension_semantics=("arbitrary", "arbitrary"), vmem_limit_bytes=56 * 1024 * 1024
        ),
        cost_estimate=pl.CostEstimate(
            flops=flops,
            bytes_accessed=4 * right_own.size * 2 + per_row * per_col * width * width * 4,
            transcendentals=0,
        ),
    )(left_ids.reshape(-1), right_ids.reshape(-1), rot, left_own, right_own, left_other, right_other)


def shift(x, axis, step):
    n = lax.axis_size(axis)
    return lax.ppermute(x, axis, [(i, (i + step) % n) for i in range(n)])


def z_ring(piece):
    from_above = shift(piece, "z", -1)
    from_below = shift(piece, "z", 1)
    half = piece.shape[0] // 2
    far_low = shift(from_below[:half], "z", 1)
    far_high = shift(from_above[half:], "z", -1)
    far = jnp.concatenate([far_low, far_high], axis=0)
    return jnp.stack([piece, from_above, far, from_below])


def ring_gather(bundle):
    from_below = shift(bundle, "y", 1)
    from_above = shift(bundle, "y", -1)
    far_low = shift(from_below[:1], "y", 1)
    far_high = shift(from_above[1:], "y", -1)
    far = jnp.concatenate([far_low, far_high], axis=0)
    return jnp.stack([bundle, from_above, far, from_below])


def local(sensitivity, tile_ids, counts, weight_class):
    row_devices = lax.axis_size("xlo") * lax.axis_size("y")
    chips = lax.axis_size("xhi") * lax.axis_size("z")
    cores = lax.axis_size("core")
    me_core = lax.axis_index("core")
    blocks, owners, slots, rows, width = sensitivity.shape
    per_row = TILES // row_devices
    per_col = per_row // cores
    live = jnp.arange(slots, dtype=jnp.int32)[None, None, :] < counts[:, :, None]
    factor = station_scale(weight_class)[:, None, None, :, None] * live[:, :, :, None, None].astype(
        jnp.float32
    )
    weighted = (sensitivity.astype(jnp.float32) * factor).astype(jnp.bfloat16)
    live_ids = jnp.where(live, tile_ids, -1).astype(jnp.bfloat16)
    band = jnp.zeros((blocks, owners, slots, BAND, width), jnp.bfloat16)
    band = band.at[:, :, :, 0, :].set(live_ids[..., None])
    tagged = jnp.concatenate([weighted, band], axis=3)
    band_rows = rows + BAND

    n_xhi = lax.axis_size("xhi")
    n_xlo = lax.axis_size("xlo")
    doubled = jnp.repeat(tagged, n_xhi, axis=1)
    left = lax.all_to_all(doubled, ("xlo", "y", "xhi"), split_axis=1, concat_axis=0, tiled=True)
    left = left.reshape(row_devices, n_xhi, slots, band_rows, width)
    left_own = z_ring(left)
    doubled = jnp.concatenate([tagged] * n_xlo, axis=1)
    right = lax.all_to_all(doubled, ("xlo", "xhi", "z"), split_axis=1, concat_axis=0, tiled=True)
    right_own = ring_gather(right.reshape(n_xlo, chips, slots, band_rows, width))
    left_other = shift(left_own, "core", 1)
    right_other = shift(right_own, "core", 1)

    n_y = lax.axis_size("y")
    n_z = lax.axis_size("z")
    me_y = lax.axis_index("y")
    me_z = lax.axis_index("z")
    me_xhi = lax.axis_index("xhi")
    absolute_y = (jnp.arange(n_y, dtype=jnp.int32) - me_y) % n_y
    k_rel = jnp.arange(n_xhi * n_z, dtype=jnp.int32)
    chip_of = (k_rel % n_xhi) * n_z + (me_z + k_rel // n_xhi) % n_z

    def ids(left_half, right_half):
        left_ids = left_half[:, :, :, :, rows, 0].astype(jnp.int32)
        left_ids = jnp.transpose(left_ids, (1, 0, 2, 3))
        right_ids = right_half[:, :, :, :, rows, 0].astype(jnp.int32) - me_core * per_col
        right_ids = jnp.transpose(right_ids[absolute_y], (1, 0, 2, 3)).reshape(row_devices, chips, slots)
        right_ids = right_ids[:, chip_of]
        right_ids = jnp.where((right_ids >= 0) & (right_ids < per_col), right_ids, -1)
        return left_ids, right_ids

    own_left_ids, own_right_ids = ids(left_own, right_own)
    other_left_ids, other_right_ids = ids(left_other, right_other)
    left_ids = jnp.stack([own_left_ids, other_left_ids])
    right_ids = jnp.stack([own_right_ids, other_right_ids])
    rot = jnp.stack([me_y, me_xhi, me_z]).astype(jnp.int32)
    return accumulate(
        left_own, right_own, left_other, right_other, left_ids, right_ids, rot, rows, per_row, per_col
    )

def solution(mesh):
    row_devices, col_devices = mesh.devices.shape
    cores = 2
    x_lo = 2
    x_hi = 2
    mesh3 = jax.sharding.Mesh(
        mesh.devices.reshape(x_lo, row_devices // x_lo, x_hi, col_devices // cores // x_hi, cores),
        ("xlo", "y", "xhi", "z", "core"),
    )
    blocks = ("xlo", "y", "xhi", "z", "core")
    in_specs = (
        P(blocks, None, None, None, None),
        P(blocks, None, None),
        P(blocks, None),
        P(blocks, None),
    )
    out_specs = P(("xlo", "y"), ("xhi", "z", "core"))
    return jax.shard_map(local, mesh=mesh3, in_specs=in_specs, out_specs=out_specs, check_vma=False)
```

```python
import functools

import jax
import jax.numpy as jnp
from jax import lax
from jax.experimental import pallas as pl
from jax.experimental.pallas import tpu as pltpu
from jax.sharding import PartitionSpec as P

TILES = 128
BAND = 16


def station_scale(weight_class):
    levels = jnp.array([1.0, 0.5, 0.25, 0.125], jnp.float32)
    hits = weight_class[..., None] == jnp.arange(4, dtype=jnp.int32)
    return jnp.sum(jnp.where(hits, levels, jnp.float32(0.0)), axis=-1)


def gram_kernel(slots, rows, width, group, lids_ref, rids_ref, rot_ref,
                left_own, right_own, left_other, right_other, out_ref):
    h = pl.program_id(0)
    r = pl.program_id(1)

    @pl.when((h == 0) & (r == 0))
    def _():
        out_ref[...] = jnp.zeros_like(out_ref)

    n_z = left_own.shape[0]
    n_xhi = left_own.shape[1]

    def run(left_ref, right_ref):
        def body(k, carry):
            b = (h * pl.num_programs(1) + r) * group + k
            z_rel = k // n_xhi
            x_abs = lax.rem(k, n_xhi)
            chip = x_abs * n_z + lax.rem(rot_ref[2] + z_rel, n_z)
            lids = [lids_ref[b * slots + i] for i in range(slots)]
            rids = [rids_ref[b * slots + j] for j in range(slots)]
            any_left = functools.reduce(jnp.logical_or, [li >= 0 for li in lids])
            any_right = functools.reduce(jnp.logical_or, [rj >= 0 for rj in rids])

            @pl.when(any_left & any_right)
            def _():
                lhs = jnp.concatenate([left_ref[z_rel, x_abs, i, :rows, :] for i in range(slots)], axis=1)
                rhs = jnp.concatenate([right_ref[chip, j, :rows, :] for j in range(slots)], axis=1)
                gram = lax.dot_general(
                    lhs, rhs, (((0,), (0,)), ((), ())), preferred_element_type=jnp.float32
                )
                for i in range(slots):
                    for j in range(slots):

                        @pl.when((lids[i] >= 0) & (rids[j] >= 0))
                        def _():
                            out_rows = pl.ds(pl.multiple_of(lids[i] * width, width), width)
                            out_cols = pl.ds(pl.multiple_of(rids[j] * width, width), width)
                            out_ref[out_rows, out_cols] += gram[i * width:(i + 1) * width, j * width:(j + 1) * width]

            return carry

        lax.fori_loop(0, group, body, 0)

    @pl.when(h == 0)
    def _():
        run(left_own, right_own)

    @pl.when(h == 1)
    def _():
        run(left_other, right_other)


def accumulate(left_own, right_own, left_other, right_other, left_ids, right_ids, rot, rows, per_row, per_col):
    n_z, n_row, n_xhi, slots, band_rows, width = left_own.shape
    n_chip = n_xhi * n_z
    n_y = right_own.shape[0]
    last = n_row - 1
    out_shape = (per_row * width, per_col * width)

    def right_block(r, rot):
        return (lax.rem(lax.rem(r, n_y) - rot[0] + n_y, n_y), r // n_y, 0, 0, 0, 0)

    left_block = (n_z, None, n_xhi, slots, band_rows, width)
    right_spec = (None, None, n_chip, slots, band_rows, width)
    in_specs = [
        pl.BlockSpec(left_block, lambda h, r, lids, rids, rot: (0, jnp.where(h == 0, r, last), 0, 0, 0, 0)),
        pl.BlockSpec(right_spec, lambda h, r, lids, rids, rot: right_block(jnp.where(h == 0, r, last), rot)),
        pl.BlockSpec(left_block, lambda h, r, lids, rids, rot: (0, jnp.where(h == 0, 0, r), 0, 0, 0, 0)),
        pl.BlockSpec(right_spec, lambda h, r, lids, rids, rot: right_block(jnp.where(h == 0, 0, r), rot)),
    ]
    grid_spec = pltpu.PrefetchScalarGridSpec(
        num_scalar_prefetch=3,
        grid=(2, n_row),
        in_specs=in_specs,
        out_specs=pl.BlockSpec(out_shape, lambda h, r, lids, rids, rot: (0, 0)),
    )
    stations = 2 * n_row * n_chip
    flops = 2 * stations * slots * slots * rows * width * width
    return pl.pallas_call(
        functools.partial(gram_kernel, slots, rows, width, n_chip),
        grid_spec=grid_spec,
        out_shape=jax.ShapeDtypeStruct(out_shape, jnp.float32),
        compiler_params=pltpu.CompilerParams(
            dimension_semantics=("arbitrary", "arbitrary"), vmem_limit_bytes=56 * 1024 * 1024
        ),
        cost_estimate=pl.CostEstimate(
            flops=flops,
            bytes_accessed=4 * right_own.size * 2 + per_row * per_col * width * width * 4,
            transcendentals=0,
        ),
    )(left_ids.reshape(-1), right_ids.reshape(-1), rot, left_own, right_own, left_other, right_other)


def shift(x, axis, step):
    n = lax.axis_size(axis)
    return lax.ppermute(x, axis, [(i, (i + step) % n) for i in range(n)])


def place(pieces, shape, dtype):
    own = jnp.zeros(shape, dtype)
    other = jnp.zeros(shape, dtype)
    for index, piece in pieces:
        own = own.at[index].set(piece)
        other = other.at[index].set(shift(piece, "core", 1))
    return own, other


def z_ring(piece):
    from_above = shift(piece, "z", -1)
    from_below = shift(piece, "z", 1)
    half = piece.shape[0] // 2
    far_low = shift(from_below[:half], "z", 1)
    far_high = shift(from_above[half:], "z", -1)
    pieces = [
        (0, piece),
        (1, from_above),
        (3, from_below),
        ((2, slice(0, half)), far_low),
        ((2, slice(half, None)), far_high),
    ]
    return place(pieces, (4,) + piece.shape, piece.dtype)


def ring_gather(bundle):
    from_below = shift(bundle, "y", 1)
    from_above = shift(bundle, "y", -1)
    far_low = shift(from_below[:1], "y", 1)
    far_high = shift(from_above[1:], "y", -1)
    pieces = [
        (0, bundle),
        (1, from_above),
        (3, from_below),
        ((2, slice(0, 1)), far_low),
        ((2, slice(1, None)), far_high),
    ]
    return place(pieces, (4,) + bundle.shape, bundle.dtype)

def local(sensitivity, tile_ids, counts, weight_class):
    row_devices = lax.axis_size("xlo") * lax.axis_size("y")
    chips = lax.axis_size("xhi") * lax.axis_size("z")
    cores = lax.axis_size("core")
    me_core = lax.axis_index("core")
    blocks, owners, slots, rows, width = sensitivity.shape
    per_row = TILES // row_devices
    per_col = per_row // cores
    live = jnp.arange(slots, dtype=jnp.int32)[None, None, :] < counts[:, :, None]
    factor = station_scale(weight_class)[:, None, None, :, None] * live[:, :, :, None, None].astype(
        jnp.float32
    )
    weighted = (sensitivity.astype(jnp.float32) * factor).astype(jnp.bfloat16)
    live_ids = jnp.where(live, tile_ids, -1).astype(jnp.bfloat16)
    band = jnp.zeros((blocks, owners, slots, BAND, width), jnp.bfloat16)
    band = band.at[:, :, :, 0, :].set(live_ids[..., None])
    tagged = jnp.concatenate([weighted, band], axis=3)
    band_rows = rows + BAND

    n_xhi = lax.axis_size("xhi")
    n_xlo = lax.axis_size("xlo")
    doubled = jnp.repeat(tagged, n_xhi, axis=1)
    left = lax.all_to_all(doubled, ("xlo", "y", "xhi"), split_axis=1, concat_axis=0, tiled=True)
    left = left.reshape(row_devices, n_xhi, slots, band_rows, width)
    left_own, left_other = z_ring(left)
    doubled = jnp.concatenate([tagged] * n_xlo, axis=1)
    right = lax.all_to_all(doubled, ("xlo", "xhi", "z"), split_axis=1, concat_axis=0, tiled=True)
    right_own, right_other = ring_gather(right.reshape(n_xlo, chips, slots, band_rows, width))

    n_y = lax.axis_size("y")
    n_z = lax.axis_size("z")
    me_y = lax.axis_index("y")
    me_z = lax.axis_index("z")
    me_xhi = lax.axis_index("xhi")
    absolute_y = (jnp.arange(n_y, dtype=jnp.int32) - me_y) % n_y
    k_rel = jnp.arange(n_xhi * n_z, dtype=jnp.int32)
    chip_of = (k_rel % n_xhi) * n_z + (me_z + k_rel // n_xhi) % n_z

    def ids(left_half, right_half):
        left_ids = left_half[:, :, :, :, rows, 0].astype(jnp.int32)
        left_ids = jnp.transpose(left_ids, (1, 0, 2, 3))
        right_ids = right_half[:, :, :, :, rows, 0].astype(jnp.int32) - me_core * per_col
        right_ids = jnp.transpose(right_ids[absolute_y], (1, 0, 2, 3)).reshape(row_devices, chips, slots)
        right_ids = right_ids[:, chip_of]
        right_ids = jnp.where((right_ids >= 0) & (right_ids < per_col), right_ids, -1)
        return left_ids, right_ids

    own_left_ids, own_right_ids = ids(left_own, right_own)
    other_left_ids, other_right_ids = ids(left_other, right_other)
    left_ids = jnp.stack([own_left_ids, other_left_ids])
    right_ids = jnp.stack([own_right_ids, other_right_ids])
    rot = jnp.stack([me_y, me_xhi, me_z]).astype(jnp.int32)
    return accumulate(
        left_own, right_own, left_other, right_other, left_ids, right_ids, rot, rows, per_row, per_col
    )

def solution(mesh):
    row_devices, col_devices = mesh.devices.shape
    cores = 2
    x_lo = 2
    x_hi = 2
    mesh3 = jax.sharding.Mesh(
        mesh.devices.reshape(x_lo, row_devices // x_lo, x_hi, col_devices // cores // x_hi, cores),
        ("xlo", "y", "xhi", "z", "core"),
    )
    blocks = ("xlo", "y", "xhi", "z", "core")
    in_specs = (
        P(blocks, None, None, None, None),
        P(blocks, None, None),
        P(blocks, None),
        P(blocks, None),
    )
    out_specs = P(("xlo", "y"), ("xhi", "z", "core"))
    return jax.shard_map(local, mesh=mesh3, in_specs=in_specs, out_specs=out_specs, check_vma=False)
```

```python
import functools

import jax
import jax.numpy as jnp
from jax import lax
from jax.experimental import pallas as pl
from jax.experimental.pallas import tpu as pltpu
from jax.sharding import PartitionSpec as P

TILES = 128
BAND = 16


def station_scale(weight_class):
    levels = jnp.array([1.0, 0.5, 0.25, 0.125], jnp.float32)
    hits = weight_class[..., None] == jnp.arange(4, dtype=jnp.int32)
    return jnp.sum(jnp.where(hits, levels, jnp.float32(0.0)), axis=-1)


def gram_kernel(slots, rows, width, group, carry_in, lids_ref, rids_ref, rot_ref, *refs):
    if carry_in:
        prev_ref, left_ref, right_ref, out_ref = refs
    else:
        left_ref, right_ref, out_ref = refs
    r = pl.program_id(0)

    @pl.when(r == 0)
    def _():
        if carry_in:
            out_ref[...] = prev_ref[...]
        else:
            out_ref[...] = jnp.zeros_like(out_ref)

    n_z = left_ref.shape[0]
    n_xhi = left_ref.shape[1]

    def body(k, carry):
        b = r * group + k
        z_rel = k // n_xhi
        x_abs = lax.rem(k, n_xhi)
        chip = x_abs * n_z + lax.rem(rot_ref[2] + z_rel, n_z)
        lids = [lids_ref[b * slots + i] for i in range(slots)]
        rids = [rids_ref[b * slots + j] for j in range(slots)]
        any_left = functools.reduce(jnp.logical_or, [li >= 0 for li in lids])
        any_right = functools.reduce(jnp.logical_or, [rj >= 0 for rj in rids])

        @pl.when(any_left & any_right)
        def _():
            lhs = jnp.concatenate([left_ref[z_rel, x_abs, i, :rows, :] for i in range(slots)], axis=1)
            rhs = jnp.concatenate([right_ref[chip, j, :rows, :] for j in range(slots)], axis=1)
            gram = lax.dot_general(
                lhs, rhs, (((0,), (0,)), ((), ())), preferred_element_type=jnp.float32
            )
            for i in range(slots):
                for j in range(slots):

                    @pl.when((lids[i] >= 0) & (rids[j] >= 0))
                    def _():
                        out_rows = pl.ds(pl.multiple_of(lids[i] * width, width), width)
                        out_cols = pl.ds(pl.multiple_of(rids[j] * width, width), width)
                        out_ref[out_rows, out_cols] += gram[i * width:(i + 1) * width, j * width:(j + 1) * width]

        return carry

    lax.fori_loop(0, group, body, 0)


def accumulate(prev, left, left_ids, right, right_ids, rot, rows, per_row, per_col):
    n_z, n_row, n_xhi, slots, band_rows, width = left.shape
    n_chip = n_xhi * n_z
    n_y = right.shape[0]
    out_shape = (per_row * width, per_col * width)

    def right_map(r, lids, rids, rot):
        return (lax.rem(lax.rem(r, n_y) - rot[0] + n_y, n_y), r // n_y, 0, 0, 0, 0)

    in_specs = [
        pl.BlockSpec((n_z, None, n_xhi, slots, band_rows, width), lambda r, lids, rids, rot: (0, r, 0, 0, 0, 0)),
        pl.BlockSpec((None, None, n_chip, slots, band_rows, width), right_map),
    ]
    operands = [left, right]
    carry_in = prev is not None
    if carry_in:
        in_specs = [pl.BlockSpec(out_shape, lambda r, lids, rids, rot: (0, 0))] + in_specs
        operands = [prev] + operands
    grid_spec = pltpu.PrefetchScalarGridSpec(
        num_scalar_prefetch=3,
        grid=(n_row,),
        in_specs=in_specs,
        out_specs=pl.BlockSpec(out_shape, lambda r, lids, rids, rot: (0, 0)),
    )
    stations = n_row * n_chip
    flops = 2 * stations * slots * slots * rows * width * width
    return pl.pallas_call(
        functools.partial(gram_kernel, slots, rows, width, n_chip, carry_in),
        grid_spec=grid_spec,
        out_shape=jax.ShapeDtypeStruct(out_shape, jnp.float32),
        input_output_aliases={3: 0} if carry_in else {},
        compiler_params=pltpu.CompilerParams(
            dimension_semantics=("arbitrary",), vmem_limit_bytes=56 * 1024 * 1024
        ),
        cost_estimate=pl.CostEstimate(
            flops=flops,
            bytes_accessed=2 * right.size * 2 + per_row * per_col * width * width * 4,
            transcendentals=0,
        ),
    )(left_ids.reshape(-1), right_ids.reshape(-1), rot, *operands)

def shift(x, axis, step):
    n = lax.axis_size(axis)
    return lax.ppermute(x, axis, [(i, (i + step) % n) for i in range(n)])


def z_ring(piece):
    from_above = shift(piece, "z", -1)
    from_below = shift(piece, "z", 1)
    half = piece.shape[0] // 2
    far_low = shift(from_below[:half], "z", 1)
    far_high = shift(from_above[half:], "z", -1)
    far = jnp.concatenate([far_low, far_high], axis=0)
    return jnp.stack([piece, from_above, far, from_below])


def ring_gather(bundle):
    from_below = shift(bundle, "y", 1)
    from_above = shift(bundle, "y", -1)
    far_low = shift(from_below[:1], "y", 1)
    far_high = shift(from_above[1:], "y", -1)
    far = jnp.concatenate([far_low, far_high], axis=0)
    return jnp.stack([bundle, from_above, far, from_below])


def exchange(slices, axes, size, kinds):
    me = 0
    for axis in axes:
        me = me * lax.axis_size(axis) + lax.axis_index(axis)
    received = [slices[lax.rem(me, kinds)]]
    for s in range(1, size):
        chunk = slices[lax.rem(me + s, kinds)]
        received.append(lax.ppermute(chunk, axes, [(i, (i + s) % size) for i in range(size)]))
    by_shift = jnp.stack(received)
    sources = jnp.arange(size, dtype=jnp.int32)
    return by_shift[lax.rem(me - sources + size, size)]


def local(sensitivity, tile_ids, counts, weight_class):
    row_devices = lax.axis_size("xlo") * lax.axis_size("y")
    chips = lax.axis_size("xhi") * lax.axis_size("z")
    cores = lax.axis_size("core")
    me_core = lax.axis_index("core")
    blocks, owners, slots, rows, width = sensitivity.shape
    per_row = TILES // row_devices
    per_col = per_row // cores
    live = jnp.arange(slots, dtype=jnp.int32)[None, None, :] < counts[:, :, None]
    factor = station_scale(weight_class)[:, None, None, :, None] * live[:, :, :, None, None].astype(
        jnp.float32
    )
    weighted = (sensitivity.astype(jnp.float32) * factor).astype(jnp.bfloat16)
    live_ids = jnp.where(live, tile_ids, -1).astype(jnp.bfloat16)
    band = jnp.zeros((blocks, owners, slots, BAND, width), jnp.bfloat16)
    band = band.at[:, :, :, 0, :].set(live_ids[..., None])
    tagged = jnp.concatenate([weighted, band], axis=3)
    band_rows = rows + BAND

    n_xhi = lax.axis_size("xhi")
    n_xlo = lax.axis_size("xlo")
    doubled = jnp.repeat(tagged, n_xhi, axis=1)
    left = lax.all_to_all(doubled, ("xlo", "y", "xhi"), split_axis=1, concat_axis=0, tiled=True)
    left = left.reshape(row_devices, n_xhi, slots, band_rows, width)
    left_own = z_ring(left)
    right = exchange(tagged[0], ("xlo", "xhi", "z"), n_xlo * chips, chips)
    right_own = ring_gather(right.reshape(n_xlo, chips, slots, band_rows, width))
    left_other = shift(left_own, "core", 1)
    right_other = shift(right_own, "core", 1)

    n_y = lax.axis_size("y")
    n_z = lax.axis_size("z")
    me_y = lax.axis_index("y")
    me_z = lax.axis_index("z")
    me_xhi = lax.axis_index("xhi")
    absolute_y = (jnp.arange(n_y, dtype=jnp.int32) - me_y) % n_y
    k_rel = jnp.arange(n_xhi * n_z, dtype=jnp.int32)
    chip_of = (k_rel % n_xhi) * n_z + (me_z + k_rel // n_xhi) % n_z

    def part(prev, left_half, right_half):
        left_ids = left_half[:, :, :, :, rows, 0].astype(jnp.int32)
        left_ids = jnp.transpose(left_ids, (1, 0, 2, 3))
        right_ids = right_half[:, :, :, :, rows, 0].astype(jnp.int32) - me_core * per_col
        right_ids = jnp.transpose(right_ids[absolute_y], (1, 0, 2, 3)).reshape(row_devices, chips, slots)
        right_ids = right_ids[:, chip_of]
        right_ids = jnp.where((right_ids >= 0) & (right_ids < per_col), right_ids, -1)
        rot = jnp.stack([me_y, me_xhi, me_z]).astype(jnp.int32)
        return accumulate(prev, left_half, left_ids, right_half, right_ids, rot, rows, per_row, per_col)

    normal = part(None, left_own, right_own)
    return part(normal, left_other, right_other)

def solution(mesh):
    row_devices, col_devices = mesh.devices.shape
    cores = 2
    x_lo = 2
    x_hi = 2
    mesh3 = jax.sharding.Mesh(
        mesh.devices.reshape(x_lo, row_devices // x_lo, x_hi, col_devices // cores // x_hi, cores),
        ("xlo", "y", "xhi", "z", "core"),
    )
    blocks = ("xlo", "y", "xhi", "z", "core")
    in_specs = (
        P(blocks, None, None, None, None),
        P(blocks, None, None),
        P(blocks, None),
        P(blocks, None),
    )
    out_specs = P(("xlo", "y"), ("xhi", "z", "core"))
    return jax.shard_map(local, mesh=mesh3, in_specs=in_specs, out_specs=out_specs, check_vma=False)
```
